32 devices in a mesh: head: 2 (over x), ctx: 16 (over z, y, core).
Axes of the slice: x: 2, y: 2, z: 4, core: 2. Of those that a mesh axis runs over, the one named last changes fastest.
Arguments:
- queries: bfloat16 [8192, 8192], P(('ctx', 'head')), may hold values from -6 to 6
- unrotated_keys: bfloat16 [8192, 1024], P(('ctx', 'head')), may hold values from -6 to 6
- value_rows: bfloat16 [8192, 1024], P(('ctx', 'head')), may hold values from -6 to 6
- outputs: bfloat16 [8192, 8192], P(('ctx', 'head')), may hold values from -6 to 6
- output_gradient: bfloat16 [8192, 8192], P(('ctx', 'head')), may hold values from -6 to 6
- saved_logsumexp: float32 [64, 8192], P(None, ('ctx', 'head')), may hold values from 4 to 6
- ancestors: int32 [16, 1], replicated, may hold values from -1 to 14, as said below
- placement: int32 [16], replicated, may hold values from 0 to 15, as said below
- positions: int32 [8192], P(('ctx', 'head')), may hold values from 0 to 8191, as said below
Outputs:
- grad_queries: bfloat16 [8192, 8192], P(('ctx', 'head'))
- grad_keys: bfloat16 [8192, 1024], P(('ctx', 'head'))
- grad_values: bfloat16 [8192, 1024], P(('ctx', 'head'))
The draws below stay inside these ranges and needn't reach their ends.
Inputs may be any that keep to these rules, and one draw needn't show every extreme that they name: Each logical block b > 0 has one parent among blocks max(0, b - 4) to b - 1; entry k of ancestors[b] is b's (k + 1)-th ancestor, -1 above the root block 0; block 15 has parent 16 - 2. `placement`: A permutation of the 16 logical blocks. `positions`: A token's position is 512 times the number of its logical block plus its offset in its block.
All inputs are finite; a program needn't handle non-finite values.
Results may differ from the reference program's by a relative error of at most 0.023.
Values may be sent and summed in bfloat16 or wider, within the bound.
No kernel may reach another device: no remote copies, remote signals or barrier semaphores. Data moves between devices by JAX's collectives and lax.ppermute only.
A program may use at most 256 MiB of HBM per device.

```python
import math
import jax
import jax.numpy as jnp
from jax import lax

D = 8192
QUERY_HEADS = 64
KEY_VALUE_HEADS = 8
HEAD_SIZE = 128
TREE_BLOCK = 512
ANC = 1
NBLK = 16
TOTAL_TOKENS = 8192


def tree_parts(key):
    base_key = jax.random.fold_in(key, 4242)
    blocks = jnp.arange(NBLK, dtype=jnp.int32)
    lowest = jnp.maximum(blocks - 4, 0)
    spread = jnp.maximum(blocks - lowest, 1)
    raw_bits = jax.random.randint(jax.random.fold_in(base_key, 1), (NBLK,), 0, 1 << 20, dtype=jnp.int32)
    parent = jnp.where(blocks == 0, -1, lowest + raw_bits % spread)
    parent = jnp.where(blocks == NBLK - 1, NBLK - 2, parent).astype(jnp.int32)
    columns = []
    current = parent
    for k in range(ANC):
        columns.append(current)
        current = jnp.where(current >= 0, parent[jnp.maximum(current, 0)], -1).astype(jnp.int32)
    ancestor_table = jnp.stack(columns, 1).astype(jnp.int32)
    order = jax.random.permutation(jax.random.fold_in(base_key, 2), NBLK).astype(jnp.int32)
    return (ancestor_table, order)


def draw_ancestors(key, part):
    ancestor_table, order = tree_parts(key)
    return ancestor_table


def draw_placement(key, part):
    ancestor_table, order = tree_parts(key)
    return order


def draw_positions(key, part):
    ancestor_table, order = tree_parts(key)
    tokens_all = jnp.arange(TOTAL_TOKENS, dtype=jnp.int32)
    slot_ids = tokens_all // TREE_BLOCK
    return (order[slot_ids] * TREE_BLOCK + tokens_all % TREE_BLOCK).astype(jnp.int32)


def steps_of(own_key, extent, pieces, least, high):
    gain = 1.0
    for dim, parts in pieces:
        draws = jax.random.uniform(jax.random.fold_in(jax.random.fold_in(own_key, 6), dim), (parts,), jnp.float32, least / len(pieces), high / len(pieces))
        gain = gain * jnp.repeat(jnp.exp(draws), extent[dim] // parts).reshape((-1,) + (1,) * (len(extent) - 1 - dim))
    return gain


def gaussian(key, dims, scale, bound, split=(), held_as=jnp.bfloat16):
    factor_of = steps_of(key, dims, split, -0.22, 0.18) if split else 1.0
    values = jax.random.normal(key, dims, jnp.float32) * scale * factor_of
    return jnp.minimum(jnp.maximum(values, -bound), bound).astype(held_as)


def setup_inputs(seed: int = 0) -> dict:
    splits = jax.random.split(jax.random.key(seed), 10)
    return {
        "queries": gaussian(splits[0], (TOTAL_TOKENS, D), 1.0, 6.0, ((0, 32),)),
        "unrotated_keys": gaussian(splits[1], (TOTAL_TOKENS, KEY_VALUE_HEADS * HEAD_SIZE), 1.0, 6.0, ((0, 32),)),
        "value_rows": gaussian(splits[2], (TOTAL_TOKENS, KEY_VALUE_HEADS * HEAD_SIZE), 1.0, 6.0, ((0, 32),)),
        "outputs": gaussian(splits[3], (TOTAL_TOKENS, D), 1.0, 6.0, ((0, 32),)),
        "output_gradient": gaussian(splits[4], (TOTAL_TOKENS, D), 1.0, 6.0, ((0, 32),)),
        "saved_logsumexp": jnp.clip(4.0 + 2.0 * jax.random.uniform(splits[5], (QUERY_HEADS, TOTAL_TOKENS), jnp.float32) ** steps_of(splits[5], (QUERY_HEADS, TOTAL_TOKENS), ((1, 32),), -0.2, 0.2), 4.0, 6.0),
        "ancestors": draw_ancestors(jax.random.fold_in(splits[9], 71), 0),
        "placement": draw_placement(jax.random.fold_in(splits[9], 71), 0),
        "positions": draw_positions(jax.random.fold_in(splits[9], 71), 0),
    }


rope_base = 500000.0

def rope_tables(positions):
    half_dim = HEAD_SIZE // 2
    freq_index = jnp.arange(half_dim, dtype=jnp.float32)
    inverse = rope_base ** (-(2.0 * freq_index / HEAD_SIZE))
    angles = positions.astype(jnp.float32)[:, None] * inverse[None, :]
    return (jnp.cos(angles), jnp.sin(angles))

def rotate(block, cosine_table, sine_table):
    row_count = block.shape[0]
    head_count = block.shape[1] // HEAD_SIZE
    half_dim = HEAD_SIZE // 2
    x = block.astype(jnp.float32).reshape(row_count, head_count, HEAD_SIZE)
    former = x[..., :half_dim]
    latter = x[..., half_dim:]
    c = cosine_table[:, None, :]
    s = sine_table[:, None, :]
    turned = jnp.concatenate([former * c - latter * s, latter * c + former * s], -1)
    return turned.reshape(row_count, head_count * HEAD_SIZE)

def unrotate(block, cosine_table, sine_table):
    row_count = block.shape[0]
    head_count = block.shape[1] // HEAD_SIZE
    half_dim = HEAD_SIZE // 2
    x = block.astype(jnp.float32).reshape(row_count, head_count, HEAD_SIZE)
    former = x[..., :half_dim]
    latter = x[..., half_dim:]
    c = cosine_table[:, None, :]
    s = sine_table[:, None, :]
    turned = jnp.concatenate([former * c + latter * s, latter * c - former * s], -1)
    return turned.reshape(row_count, head_count * HEAD_SIZE)

def row_products(grads, outs):
    row_count = grads.shape[0]
    head_count = grads.shape[1] // HEAD_SIZE
    product = grads.astype(jnp.float32) * outs.astype(jnp.float32)
    return lax.optimization_barrier(jnp.sum(product.reshape(row_count, head_count, HEAD_SIZE), -1)).T

def tile_grads(query_block_tile, gradient_tile, logsumexp_tile, delta_block_tile, key_block_tile, value_block_tile, allowed):
    score_scale = 1.0 / math.sqrt(HEAD_SIZE)
    query_f = query_block_tile.astype(jnp.float32)
    grad_f = gradient_tile.astype(jnp.float32)
    key_f = key_block_tile.astype(jnp.float32)
    value_f = value_block_tile.astype(jnp.float32)
    scores = score_scale * jnp.einsum('qkgd,skd->kgqs', query_f, key_f)
    probability = jnp.where(allowed[None, None], jnp.exp(scores - logsumexp_tile[..., None]), 0.0)
    grad_prob = jnp.einsum('qkgd,skd->kgqs', grad_f, value_f)
    grad_score = probability * (grad_prob - delta_block_tile[..., None])
    prob_half = lax.optimization_barrier(probability.astype(jnp.bfloat16)).astype(jnp.float32)
    score_half = lax.optimization_barrier(grad_score.astype(jnp.bfloat16)).astype(jnp.float32)
    grad_v = jnp.einsum('kgqs,qkgd->skd', prob_half, grad_f)
    grad_k = score_scale * jnp.einsum('kgqs,qkgd->skd', score_half, query_f)
    grad_q = score_scale * jnp.einsum('kgqs,skd->qkgd', score_half, key_f)
    return (grad_q, grad_k, grad_v)

def reference(queries, unrotated_keys, value_rows, outputs, output_gradient, saved_logsumexp, ancestors, placement, positions):
    query_group = QUERY_HEADS // KEY_VALUE_HEADS
    cosine_table, sine_table = rope_tables(positions)
    rotated_query_rows = rotate(queries, cosine_table, sine_table).astype(jnp.bfloat16)
    rotated_key_rows = rotate(unrotated_keys, cosine_table, sine_table).astype(jnp.bfloat16)
    row_delta_values = row_products(output_gradient, outputs)
    slot_of = jnp.zeros((NBLK,), jnp.int32).at[placement].set(jnp.arange(NBLK, dtype=jnp.int32))
    offsets = jnp.arange(TREE_BLOCK, dtype=jnp.int32)
    causal = offsets[None, :] <= offsets[:, None]
    key_span_width = KEY_VALUE_HEADS * HEAD_SIZE

    def one_block(state_pair, block_slot):
        key_grads, value_grads = state_pair
        first_row_index = (block_slot * TREE_BLOCK).astype(jnp.int32)
        query_block_tile = lax.dynamic_slice_in_dim(rotated_query_rows, first_row_index, TREE_BLOCK, 0).reshape(TREE_BLOCK, KEY_VALUE_HEADS, query_group, HEAD_SIZE)
        gradient_tile = lax.dynamic_slice_in_dim(output_gradient, first_row_index, TREE_BLOCK, 0).reshape(TREE_BLOCK, KEY_VALUE_HEADS, query_group, HEAD_SIZE)
        logsumexp_tile = lax.dynamic_slice_in_dim(saved_logsumexp, first_row_index, TREE_BLOCK, 1).reshape(KEY_VALUE_HEADS, query_group, TREE_BLOCK)
        delta_block_tile = lax.dynamic_slice_in_dim(row_delta_values, first_row_index, TREE_BLOCK, 1).reshape(KEY_VALUE_HEADS, query_group, TREE_BLOCK)
        chain = ancestors[placement[block_slot]]
        key_slots = jnp.concatenate([block_slot[None], slot_of[jnp.maximum(chain, 0)]]).astype(jnp.int32)
        present = jnp.concatenate([jnp.ones((1,), bool), chain >= 0])
        query_gradient = jnp.zeros((TREE_BLOCK, KEY_VALUE_HEADS, query_group, HEAD_SIZE), jnp.float32)
        for j in range(ANC + 1):
            key_first_index = (key_slots[j] * TREE_BLOCK).astype(jnp.int32)
            key_block_tile = lax.dynamic_slice_in_dim(rotated_key_rows, key_first_index, TREE_BLOCK, 0).reshape(TREE_BLOCK, KEY_VALUE_HEADS, HEAD_SIZE)
            value_block_tile = lax.dynamic_slice_in_dim(value_rows, key_first_index, TREE_BLOCK, 0).reshape(TREE_BLOCK, KEY_VALUE_HEADS, HEAD_SIZE)
            if j == 0:
                allowed = causal
            else:
                allowed = jnp.broadcast_to(present[j], (TREE_BLOCK, TREE_BLOCK))
            grad_q, grad_k, grad_v = tile_grads(query_block_tile, gradient_tile, logsumexp_tile, delta_block_tile, key_block_tile, value_block_tile, allowed)
            query_gradient = query_gradient + grad_q
            old_k = lax.dynamic_slice_in_dim(key_grads, key_first_index, TREE_BLOCK, 0)
            key_grads = lax.dynamic_update_slice_in_dim(key_grads, old_k + grad_k.reshape(TREE_BLOCK, key_span_width), key_first_index, 0)
            old_v = lax.dynamic_slice_in_dim(value_grads, key_first_index, TREE_BLOCK, 0)
            value_grads = lax.dynamic_update_slice_in_dim(value_grads, old_v + grad_v.reshape(TREE_BLOCK, key_span_width), key_first_index, 0)
        return ((key_grads, value_grads), query_gradient)
    start_pair = (jnp.zeros((TOTAL_TOKENS, key_span_width), jnp.float32), jnp.zeros((TOTAL_TOKENS, key_span_width), jnp.float32))
    (key_grads, value_grads), query_grads = lax.scan(one_block, start_pair, jnp.arange(NBLK, dtype=jnp.int32))
    rot_dq = query_grads.reshape(TOTAL_TOKENS, D).astype(jnp.bfloat16)
    rot_dk = key_grads.astype(jnp.bfloat16)
    grad_queries = unrotate(rot_dq, cosine_table, sine_table).astype(jnp.bfloat16)
    grad_keys = unrotate(rot_dk, cosine_table, sine_table).astype(jnp.bfloat16)
    grad_values = value_grads.astype(jnp.bfloat16)
    return (grad_queries, grad_keys, grad_values)
```

```python
import functools
import math

import jax
import jax.numpy as jnp
from jax import lax
from jax.experimental import pallas as pl
from jax.experimental.pallas import tpu as pltpu
from jax.sharding import PartitionSpec as P

HEAD_SIZE = 128
TREE_BLOCK = 512
LOG2E = math.log2(math.e)
LN2 = math.log(2.0)
SCALE = 1.0 / math.sqrt(HEAD_SIZE)
rope_base = 500000.0
VMEM_LIMIT = 60 * 1024 * 1024
NT = (((1,), (1,)), ((), ()))
NN = (((1,), (0,)), ((), ()))
TN = (((0,), (0,)), ((), ()))


def rope_tables(positions):
    half_dim = HEAD_SIZE // 2
    freq_index = jnp.arange(half_dim, dtype=jnp.float32)
    inverse = rope_base ** (-(2.0 * freq_index / HEAD_SIZE))
    angles = positions.astype(jnp.float32)[:, None] * inverse[None, :]
    c, s = jnp.cos(angles), jnp.sin(angles)
    return jnp.concatenate([c, c], -1), jnp.concatenate([-s, s], -1)


def dot(a, b, dims):
    return lax.dot_general(a, b, dims, preferred_element_type=jnp.float32)


def turn(x, c, s):
    return x * c + pltpu.roll(x, HEAD_SIZE // 2, 1) * s


def turn_back(x, c, s):
    return x * c - pltpu.roll(x, HEAD_SIZE // 2, 1) * s


def params(n=1):
    return pltpu.CompilerParams(
        dimension_semantics=("arbitrary",) * n, vmem_limit_bytes=VMEM_LIMIT
    )


def pack_kernel(k_ref, v_ref, c_ref, s_ref, o_ref):
    c, s = c_ref[...], s_ref[...]
    for g in range(k_ref.shape[1] // HEAD_SIZE):
        a, b = g * HEAD_SIZE, 2 * g * HEAD_SIZE
        x = k_ref[:, a : a + HEAD_SIZE].astype(jnp.float32)
        o_ref[:, b : b + HEAD_SIZE] = turn(x, c, s).astype(jnp.bfloat16)
        o_ref[:, b + HEAD_SIZE : b + 2 * HEAD_SIZE] = v_ref[:, a : a + HEAD_SIZE]


def pack(keys, values, c, s):
    rows, width = keys.shape
    return pl.pallas_call(
        pack_kernel,
        out_shape=jax.ShapeDtypeStruct((rows, 2 * width), jnp.bfloat16),
        compiler_params=params(0),
        name="pack",
    )(keys, values, c, s)


def pick_kernel(source_ref, x_ref, o_ref):
    for d in range(x_ref.shape[0]):
        o_ref[d] = x_ref[source_ref[d]]


def pick(source, x):
    return pl.pallas_call(
        pick_kernel,
        out_shape=jax.ShapeDtypeStruct(x.shape, x.dtype),
        in_specs=[
            pl.BlockSpec(memory_space=pltpu.SMEM),
            pl.BlockSpec(memory_space=pltpu.VMEM),
        ],
        out_specs=pl.BlockSpec(memory_space=pltpu.VMEM),
        compiler_params=params(0),
        name="pick",
    )(source, x)


def merge_kernel(source_ref, present_ref, x_ref, o_ref, acc_ref):
    acc_ref[...] = jnp.zeros_like(acc_ref)
    for d in range(x_ref.shape[0]):

        @pl.when(present_ref[d] != 0)
        def _():
            acc_ref[source_ref[d]] += x_ref[d].astype(jnp.float32)

    o_ref[...] = acc_ref[...].astype(o_ref.dtype)


def merge(source, present, x):
    return pl.pallas_call(
        merge_kernel,
        out_shape=jax.ShapeDtypeStruct(x.shape, x.dtype),
        in_specs=[
            pl.BlockSpec(memory_space=pltpu.SMEM),
            pl.BlockSpec(memory_space=pltpu.SMEM),
            pl.BlockSpec(memory_space=pltpu.VMEM),
        ],
        out_specs=pl.BlockSpec(memory_space=pltpu.VMEM),
        scratch_shapes=[pltpu.VMEM(x.shape, jnp.float32)],
        compiler_params=params(0),
        name="merge",
    )(source, present, x)


def tile(rq, do, lse, delta, k, v, mask):
    scores = dot(k, rq, NT)
    prob = jnp.exp2(scores - lse)
    if mask is not None:
        prob = jnp.where(mask, prob, 0.0)
    grad_score = prob * (dot(v, do, NT) - delta)
    prob_half = prob.astype(jnp.bfloat16)
    score_half = grad_score.astype(jnp.bfloat16)
    return (
        dot(score_half, k, TN),
        dot(score_half, rq, NN),
        dot(prob_half, do, NN),
    )


def own_kernel(hops, group, index_ref, q_ref, do_ref, out_ref, lse_ref, c_ref, s_ref, *refs):
    kv_refs = refs[:hops]
    rq_ref, delta_ref, dq_ref = refs[hops : hops + 3]
    dkv_refs = refs[hops + 3 : 2 * hops + 3]
    acc_refs = refs[2 * hops + 3 :]
    rows = q_ref.shape[0]
    me = index_ref[0]
    c, s = c_ref[...] * (SCALE * LOG2E), s_ref[...] * (SCALE * LOG2E)
    key_at = lax.broadcasted_iota(jnp.int32, (rows, rows), 0)
    query_at = lax.broadcasted_iota(jnp.int32, (rows, rows), 1)
    causal = key_at <= query_at
    for h in range(group):
        cols = slice(h * HEAD_SIZE, (h + 1) * HEAD_SIZE)
        do = do_ref[:, cols]
        rq_ref[:, cols] = turn(q_ref[:, cols].astype(jnp.float32), c, s).astype(jnp.bfloat16)
        product = do.astype(jnp.float32) * out_ref[:, cols].astype(jnp.float32)
        delta_ref[h : h + 1, :] = jnp.sum(product.T, axis=0, keepdims=True)

    def hop(n, mask):
        k = kv_refs[n][:, :HEAD_SIZE]
        v = kv_refs[n][:, HEAD_SIZE:]
        for h in range(group):
            cols = slice(h * HEAD_SIZE, (h + 1) * HEAD_SIZE)
            gq, gk, gv = tile(
                rq_ref[:, cols],
                do_ref[:, cols],
                lse_ref[h : h + 1, :] * LOG2E,
                delta_ref[h : h + 1, :],
                k,
                v,
                mask,
            )
            if n == 0:
                dq_ref[:, cols] = gq
            else:
                dq_ref[:, cols] += gq
            if h == 0:
                acc_refs[0][...] = gk
                acc_refs[1][...] = gv
            else:
                acc_refs[0][...] += gk
                acc_refs[1][...] += gv
        dkv_refs[n][:, :HEAD_SIZE] = (acc_refs[0][...] * LN2).astype(dkv_refs[n].dtype)
        dkv_refs[n][:, HEAD_SIZE:] = acc_refs[1][...].astype(dkv_refs[n].dtype)

    hop(0, causal)
    for n in range(1, hops):
        pl.when(me >= n)(functools.partial(hop, n, None))

        @pl.when(me < n)
        def _():
            dkv_refs[n][...] = jnp.zeros_like(dkv_refs[n])


def own(index, q, do, out, lse, c, s, kvs):
    rows, width = q.shape
    kv_count = kvs[0].shape[1] // (2 * HEAD_SIZE)
    group = width // HEAD_SIZE // kv_count
    wide = group * HEAD_SIZE
    hops = len(kvs)
    heads = kv_count * group
    big = pl.BlockSpec((rows, wide), lambda g, i: (0, g))
    row = pl.BlockSpec((group, rows), lambda g, i: (g, 0))
    table = pl.BlockSpec((rows, HEAD_SIZE), lambda g, i: (0, 0))
    pair = pl.BlockSpec((rows, 2 * HEAD_SIZE), lambda g, i: (0, g))
    tiles = heads * rows * rows * HEAD_SIZE * 10
    return pl.pallas_call(
        functools.partial(own_kernel, hops, group),
        out_shape=[
            jax.ShapeDtypeStruct((rows, width), jnp.bfloat16),
            jax.ShapeDtypeStruct((heads, rows), jnp.float32),
            jax.ShapeDtypeStruct((rows, width), jnp.float32),
            jax.ShapeDtypeStruct(kvs[0].shape, jnp.float32),
        ]
        + [jax.ShapeDtypeStruct(kvs[0].shape, jnp.bfloat16)] * (hops - 1),
        grid_spec=pltpu.PrefetchScalarGridSpec(
            num_scalar_prefetch=1,
            grid=(kv_count,),
            in_specs=[big, big, big, row, table, table] + [pair] * hops,
            out_specs=[big, row, big] + [pair] * hops,
            scratch_shapes=[pltpu.VMEM((rows, HEAD_SIZE), jnp.float32)] * 2,
        ),
        compiler_params=params(),
        cost_estimate=pl.CostEstimate(
            flops=2 * tiles * hops, bytes_accessed=rows * width * 12, transcendentals=0
        ),
        name="own",
    )(index, q, do, out, lse, c, s, *kvs)


def parent_kernel(hops, group, present_ref, rq_ref, do_ref, lse_ref, delta_ref, c_ref, s_ref, dq_in_ref, *refs):
    kv_refs = refs[:hops]
    dq_ref = refs[hops]
    dkv_refs = refs[hops + 1 : 2 * hops + 1]
    acc_refs = refs[2 * hops + 1 :]
    c, s = c_ref[...] * SCALE, s_ref[...] * SCALE

    @pl.when(present_ref[0] != 0)
    def _():
        for h in range(group):
            cols = slice(h * HEAD_SIZE, (h + 1) * HEAD_SIZE)
            total = dq_in_ref[:, cols]
            for n in range(hops):
                gq, gk, gv = tile(
                    rq_ref[:, cols],
                    do_ref[:, cols],
                    lse_ref[h : h + 1, :] * LOG2E,
                    delta_ref[h : h + 1, :],
                    kv_refs[n][:, :HEAD_SIZE],
                    kv_refs[n][:, HEAD_SIZE:],
                    None,
                )
                total += gq
                if h == 0:
                    acc_refs[0][n] = gk
                    acc_refs[1][n] = gv
                else:
                    acc_refs[0][n] += gk
                    acc_refs[1][n] += gv
            dq_ref[:, cols] = turn_back(total, c, s).astype(jnp.bfloat16)
        for n in range(hops):
            dkv_refs[n][:, :HEAD_SIZE] = (acc_refs[0][n] * LN2).astype(jnp.bfloat16)
            dkv_refs[n][:, HEAD_SIZE:] = acc_refs[1][n].astype(jnp.bfloat16)

    @pl.when(present_ref[0] == 0)
    def _():
        for h in range(group):
            cols = slice(h * HEAD_SIZE, (h + 1) * HEAD_SIZE)
            dq_ref[:, cols] = turn_back(dq_in_ref[:, cols], c, s).astype(jnp.bfloat16)
        for n in range(hops):
            dkv_refs[n][...] = jnp.zeros_like(dkv_refs[n])


def parent(present, rq, do, lse, delta, c, s, dq, kvs):
    rows, width = rq.shape
    kv_count = kvs[0].shape[1] // (2 * HEAD_SIZE)
    group = width // HEAD_SIZE // kv_count
    wide = group * HEAD_SIZE
    hops = len(kvs)
    heads = kv_count * group
    big = pl.BlockSpec((rows, wide), lambda g, i: (0, g))
    row = pl.BlockSpec((group, rows), lambda g, i: (g, 0))
    table = pl.BlockSpec((rows, HEAD_SIZE), lambda g, i: (0, 0))
    pair = pl.BlockSpec((rows, 2 * HEAD_SIZE), lambda g, i: (0, g))
    tiles = heads * rows * rows * HEAD_SIZE * 10
    return pl.pallas_call(
        functools.partial(parent_kernel, hops, group),
        out_shape=[jax.ShapeDtypeStruct((rows, width), jnp.bfloat16)]
        + [jax.ShapeDtypeStruct(kvs[0].shape, jnp.bfloat16)] * hops,
        grid_spec=pltpu.PrefetchScalarGridSpec(
            num_scalar_prefetch=1,
            grid=(kv_count,),
            in_specs=[big, big, row, row, table, table, big] + [pair] * hops,
            out_specs=[big] + [pair] * hops,
            scratch_shapes=[pltpu.VMEM((hops, rows, HEAD_SIZE), jnp.float32)] * 2,
        ),
        compiler_params=params(),
        cost_estimate=pl.CostEstimate(
            flops=2 * tiles * hops, bytes_accessed=rows * width * 10, transcendentals=0
        ),
        name="parent",
    )(present, rq, do, lse, delta, c, s, dq, *kvs)


def finish_kernel(parts, own_ref, c_ref, s_ref, *refs):
    in_refs = refs[:parts]
    dk_ref, dv_ref = refs[parts:]
    c, s = c_ref[...], s_ref[...]
    for g in range(dk_ref.shape[1] // HEAD_SIZE):
        a, b = g * HEAD_SIZE, 2 * g * HEAD_SIZE
        total = own_ref[:, b : b + 2 * HEAD_SIZE]
        for ref in in_refs:
            total = total + ref[:, b : b + 2 * HEAD_SIZE].astype(jnp.float32)
        gk = total[:, :HEAD_SIZE]
        dk_ref[:, a : a + HEAD_SIZE] = turn_back(gk, c, s).astype(jnp.bfloat16)
        dv_ref[:, a : a + HEAD_SIZE] = total[:, HEAD_SIZE:].astype(jnp.bfloat16)


def finish(local, parts, c, s):
    rows, width = local.shape
    return pl.pallas_call(
        functools.partial(finish_kernel, len(parts)),
        out_shape=[jax.ShapeDtypeStruct((rows, width // 2), jnp.bfloat16)] * 2,
        compiler_params=params(0),
        name="finish",
    )(local, c, s, *parts)


def body(
    queries,
    unrotated_keys,
    value_rows,
    outputs,
    output_gradient,
    saved_logsumexp,
    ancestors,
    placement,
    positions,
):
    hops = lax.axis_size("head")
    places = lax.axis_size("ctx")
    here = lax.axis_index("ctx")
    me = lax.axis_index("head")
    rows = queries.shape[0]
    assert rows * hops == TREE_BLOCK and placement.shape[0] == places
    c, s = rope_tables(positions)

    match = ancestors[placement][:, :1] == placement[None, :]
    source = jnp.argmax(match, axis=1).astype(jnp.int32)
    present = jnp.any(match, axis=1).astype(jnp.int32)

    kv = pack(unrotated_keys, value_rows, c, s)
    width = kv.shape[1]
    spread = (places, rows // places, width)

    def exchange(x):
        return lax.all_to_all(x.reshape(spread), "ctx", 0, 0, tiled=True)

    def shift(x, n, wrap):
        route = [(i, (i + n) % hops) for i in range(hops) if wrap or 0 <= i + n < hops]
        return lax.ppermute(x, "head", route)

    middle = exchange(kv)
    own_kv = [kv] + [shift(kv, n, False) for n in range(1, hops)]
    near = exchange(pick(source, middle)).reshape(rows, width)
    parent_kv = [near] + [shift(near, n, True) for n in range(1, hops)]

    rq, delta, dq, *own_dkv = own(
        me.astype(jnp.int32)[None], queries, output_gradient, outputs, saved_logsumexp, c, s, own_kv
    )
    grad_queries, *parent_dkv = parent(
        present[here][None], rq, output_gradient, saved_logsumexp, delta, c, s, dq, parent_kv
    )
    own_back = [shift(own_dkv[n], -n, False) for n in range(1, hops)]
    total = parent_dkv[0].astype(jnp.float32)
    for n in range(1, hops):
        total = total + shift(parent_dkv[n], -n, True).astype(jnp.float32)
    merged = merge(source, present, exchange(total.astype(jnp.bfloat16)))
    children = exchange(merged).reshape(rows, width)
    grad_keys, grad_values = finish(own_dkv[0], own_back + [children], c, s)
    return (grad_queries, grad_keys, grad_values)


def solution(mesh):
    return jax.shard_map(
        body,
        mesh=mesh,
        in_specs=(
            P(("ctx", "head"), None),
            P(("ctx", "head"), None),
            P(("ctx", "head"), None),
            P(("ctx", "head"), None),
            P(("ctx", "head"), None),
            P(None, ("ctx", "head")),
            P(),
            P(),
            P(("ctx", "head")),
        ),
        out_specs=(P(("ctx", "head"), None), P(("ctx", "head"), None), P(("ctx", "head"), None)),
        check_vma=False,
    )
```

```python
import functools
import math

import jax
import jax.numpy as jnp
from jax import lax
from jax.experimental import pallas as pl
from jax.experimental.pallas import tpu as pltpu
from jax.sharding import PartitionSpec as P


HEAD_SIZE = 128
TREE_BLOCK = 512
LOG2E = math.log2(math.e)
LN2 = math.log(2.0)
SCALE = 1.0 / math.sqrt(HEAD_SIZE)
rope_base = 500000.0
VMEM_LIMIT = 60 * 1024 * 1024
NT = (((1,), (1,)), ((), ()))
NN = (((1,), (0,)), ((), ()))
TN = (((0,), (0,)), ((), ()))


def rope_tables(positions):
    half_dim = HEAD_SIZE // 2
    freq_index = jnp.arange(half_dim, dtype=jnp.float32)
    inverse = rope_base ** (-(2.0 * freq_index / HEAD_SIZE))
    angles = positions.astype(jnp.float32)[:, None] * inverse[None, :]
    c, s = jnp.cos(angles), jnp.sin(angles)
    return jnp.concatenate([c, c], -1), jnp.concatenate([-s, s], -1)


def dot(a, b, dims):
    return lax.dot_general(a, b, dims, preferred_element_type=jnp.float32)


def turn(x, c, s):
    return x * c + pltpu.roll(x, HEAD_SIZE // 2, 1) * s


def turn_back(x, c, s):
    return x * c - pltpu.roll(x, HEAD_SIZE // 2, 1) * s


def params(n=1):
    return pltpu.CompilerParams(
        dimension_semantics=("arbitrary",) * n, vmem_limit_bytes=VMEM_LIMIT
    )


def pack_kernel(sizes, k_ref, v_ref, c_ref, s_ref, *o_refs):
    c, s = c_ref[...], s_ref[...]
    g = 0
    for size, o_ref in zip(sizes, o_refs):
        for i in range(size):
            a, b = g * HEAD_SIZE, 2 * i * HEAD_SIZE
            x = k_ref[:, a : a + HEAD_SIZE].astype(jnp.float32)
            o_ref[:, b : b + HEAD_SIZE] = turn(x, c, s).astype(jnp.bfloat16)
            o_ref[:, b + HEAD_SIZE : b + 2 * HEAD_SIZE] = v_ref[:, a : a + HEAD_SIZE]
            g += 1


def pack(sizes, keys, values, c, s):
    rows = keys.shape[0]
    return pl.pallas_call(
        functools.partial(pack_kernel, sizes),
        out_shape=[
            jax.ShapeDtypeStruct((rows, 2 * size * HEAD_SIZE), jnp.bfloat16) for size in sizes
        ],
        compiler_params=params(0),
        name="pack",
    )(keys, values, c, s)


def pick_kernel(source_ref, x_ref, o_ref):
    for d in range(x_ref.shape[0]):
        o_ref[d] = x_ref[source_ref[d]]


def pick(source, x):
    return pl.pallas_call(
        pick_kernel,
        out_shape=jax.ShapeDtypeStruct(x.shape, x.dtype),
        in_specs=[
            pl.BlockSpec(memory_space=pltpu.SMEM),
            pl.BlockSpec(memory_space=pltpu.VMEM),
        ],
        out_specs=pl.BlockSpec(memory_space=pltpu.VMEM),
        compiler_params=params(0),
        name="pick",
    )(source, x)


def merge_kernel(source_ref, present_ref, x_ref, o_ref, acc_ref):
    acc_ref[...] = jnp.zeros_like(acc_ref)
    for d in range(x_ref.shape[0]):

        @pl.when(present_ref[d] != 0)
        def _():
            acc_ref[source_ref[d]] += x_ref[d].astype(jnp.float32)

    o_ref[...] = acc_ref[...].astype(o_ref.dtype)


def merge(source, present, x):
    return pl.pallas_call(
        merge_kernel,
        out_shape=jax.ShapeDtypeStruct(x.shape, x.dtype),
        in_specs=[
            pl.BlockSpec(memory_space=pltpu.SMEM),
            pl.BlockSpec(memory_space=pltpu.SMEM),
            pl.BlockSpec(memory_space=pltpu.VMEM),
        ],
        out_specs=pl.BlockSpec(memory_space=pltpu.VMEM),
        scratch_shapes=[pltpu.VMEM(x.shape, jnp.float32)],
        compiler_params=params(0),
        name="merge",
    )(source, present, x)


def fronts(rq, do, lse, delta, k, v, mask=None):
    prob = jnp.exp2(dot(k, rq, NT) - lse)
    if mask is not None:
        prob = jnp.where(mask, prob, 0.0)
    grad_score = prob * (dot(v, do, NT) - delta)
    return prob.astype(jnp.bfloat16), grad_score.astype(jnp.bfloat16)


def stacked(ref, group):
    return jnp.concatenate([ref[:, cols_of(h)] for h in range(group)], 0)


def heads_of(width, kv_count):
    return width // HEAD_SIZE // kv_count


def cols_of(h):
    return slice(h * HEAD_SIZE, (h + 1) * HEAD_SIZE)


def diagonal_kernel(group, q_ref, do_ref, out_ref, lse_ref, c_ref, s_ref, kv_ref, rq_ref, delta_ref, dq_ref, dkv_ref, p_ref, ds_ref):
    rows = q_ref.shape[0]
    c, s = c_ref[...] * (SCALE * LOG2E), s_ref[...] * (SCALE * LOG2E)
    key_at = lax.broadcasted_iota(jnp.int32, (rows, rows), 0)
    query_at = lax.broadcasted_iota(jnp.int32, (rows, rows), 1)
    causal = key_at <= query_at
    k = kv_ref[:, :HEAD_SIZE]
    v = kv_ref[:, HEAD_SIZE:]
    for h in range(group):
        cols, lanes = cols_of(h), slice(h * rows, (h + 1) * rows)
        do = do_ref[:, cols]
        rq = turn(q_ref[:, cols].astype(jnp.float32), c, s).astype(jnp.bfloat16)
        rq_ref[:, cols] = rq
        product = do.astype(jnp.float32) * out_ref[:, cols].astype(jnp.float32)
        delta = jnp.sum(product.T, axis=0, keepdims=True)
        delta_ref[h : h + 1, :] = delta
        p_ref[:, lanes], ds_ref[:, lanes] = fronts(
            rq, do, lse_ref[h : h + 1, :] * LOG2E, delta, k, v, causal
        )
    dkv_ref[:, :HEAD_SIZE] = dot(ds_ref[...], stacked(rq_ref, group), NN) * LN2
    dkv_ref[:, HEAD_SIZE:] = dot(p_ref[...], stacked(do_ref, group), NN)
    for h in range(group):
        dq_ref[:, cols_of(h)] = dot(ds_ref[:, h * rows : (h + 1) * rows], k, TN)


def diagonal(first, count, kv_count, q, do, out, lse, c, s, kv):
    rows, width = q.shape
    group = heads_of(width, kv_count)
    wide = group * HEAD_SIZE
    big = pl.BlockSpec((rows, wide), lambda g: (0, g + first))
    row = pl.BlockSpec((group, rows), lambda g: (g + first, 0))
    table = pl.BlockSpec((rows, HEAD_SIZE), lambda g: (0, 0))
    pair = pl.BlockSpec((rows, 2 * HEAD_SIZE), lambda g: (0, g))
    part = pl.BlockSpec((rows, wide), lambda g: (0, g))
    part_row = pl.BlockSpec((group, rows), lambda g: (g, 0))
    return pl.pallas_call(
        functools.partial(diagonal_kernel, group),
        out_shape=[
            jax.ShapeDtypeStruct((rows, count * wide), jnp.bfloat16),
            jax.ShapeDtypeStruct((count * group, rows), jnp.float32),
            jax.ShapeDtypeStruct((rows, count * wide), jnp.float32),
            jax.ShapeDtypeStruct((rows, count * 2 * HEAD_SIZE), jnp.float32),
        ],
        grid=(count,),
        in_specs=[big, big, big, row, table, table, pair],
        out_specs=[part, part_row, part, pair],
        scratch_shapes=[pltpu.VMEM((rows, group * rows), jnp.bfloat16)] * 2,
        compiler_params=params(),
        cost_estimate=pl.CostEstimate(
            flops=20 * count * group * rows * rows * HEAD_SIZE,
            bytes_accessed=rows * count * wide * 12,
            transcendentals=0,
        ),
        name="diagonal",
    )(q, do, out, lse, c, s, kv)


def cross_kernel(group, joint, final, flag_ref, rq_ref, do_ref, lse_ref, delta_ref, c_ref, s_ref, dq_in_ref, *refs):
    sets = len(joint)
    refs = list(refs)
    kv_refs = [refs.pop(0) for _ in range(sum(joint))]
    if final == 2:
        refs.pop(0)
    dq_ref = refs.pop(0)
    dkv_refs = [refs.pop(0) for _ in range(sum(joint))]
    p_ref, ds_ref, k_ref, v_ref = refs[:4]
    total_ref = refs[4] if final else dq_ref
    rows = rq_ref.shape[0]
    c, s = c_ref[...] * SCALE, s_ref[...] * SCALE

    def put(cols, total):
        if final and sets == 1:
            dq_ref[:, cols] = turn_back(total, c, s).astype(jnp.bfloat16)
        else:
            total_ref[:, cols] = total

    def run(members, fresh):
        here = slice(0, len(members) * rows)
        for n, m in enumerate(members):
            k_ref[n * rows : (n + 1) * rows] = kv_refs[m][:, :HEAD_SIZE]
            v_ref[n * rows : (n + 1) * rows] = kv_refs[m][:, HEAD_SIZE:]
        k = k_ref[here]
        for h in range(group):
            lanes = slice(h * rows, (h + 1) * rows)
            p_ref[here, lanes], ds_ref[here, lanes] = fronts(
                rq_ref[:, cols_of(h)],
                do_ref[:, cols_of(h)],
                lse_ref[h : h + 1, :] * LOG2E,
                delta_ref[h : h + 1, :],
                k,
                v_ref[here],
            )
        gk = dot(ds_ref[here], stacked(rq_ref, group), NN) * LN2
        gv = dot(p_ref[here], stacked(do_ref, group), NN)
        for n, m in enumerate(members):
            own = slice(n * rows, (n + 1) * rows)
            dkv_refs[m][:, :HEAD_SIZE] = gk[own].astype(jnp.bfloat16)
            dkv_refs[m][:, HEAD_SIZE:] = gv[own].astype(jnp.bfloat16)
        for h in range(group):
            cols = cols_of(h)
            before = dq_in_ref[:, cols] if fresh else total_ref[:, cols]
            put(cols, before + dot(ds_ref[here, h * rows : (h + 1) * rows], k, TN))

    def skip(members, fresh):
        if fresh:
            for h in range(group):
                put(cols_of(h), dq_in_ref[:, cols_of(h)])
        for m in members:
            dkv_refs[m][...] = jnp.zeros_like(dkv_refs[m])

    start = 0
    for i, size in enumerate(joint):
        members = tuple(range(start, start + size))
        start += size
        pl.when(flag_ref[i] != 0)(functools.partial(run, members, i == 0))
        pl.when(flag_ref[i] == 0)(functools.partial(skip, members, i == 0))
    if final and sets > 1:
        for h in range(group):
            cols = cols_of(h)
            dq_ref[:, cols] = turn_back(total_ref[:, cols], c, s).astype(jnp.bfloat16)


def cross(first, count, kv_count, flags, joint, rq, do, lse, delta, c, s, dq, kvs, whole=None, final=False):
    rows, width = do.shape
    group = heads_of(width, kv_count)
    wide = group * HEAD_SIZE
    most = max(joint)
    big = pl.BlockSpec((rows, wide), lambda g, i: (0, g + first))
    row = pl.BlockSpec((group, rows), lambda g, i: (g + first, 0))
    table = pl.BlockSpec((rows, HEAD_SIZE), lambda g, i: (0, 0))
    pair = pl.BlockSpec((rows, 2 * HEAD_SIZE), lambda g, i: (0, g))
    part = pl.BlockSpec((rows, wide), lambda g, i: (0, g))
    part_row = pl.BlockSpec((group, rows), lambda g, i: (g, 0))
    args = [flags, rq, do, lse, delta, c, s, dq, *kvs]
    in_specs = [part, big, row, part_row, table, table, part] + [pair] * len(kvs)
    mode = 0
    aliases = {}
    if final:
        mode = 1
        if whole is not None:
            mode = 2
            aliases = {len(args): 0}
            args.append(whole)
            in_specs.append(pl.BlockSpec(memory_space=pl.ANY))
    dq_shape = (
        jax.ShapeDtypeStruct((rows, width), jnp.bfloat16)
        if final
        else jax.ShapeDtypeStruct(dq.shape, jnp.float32)
    )
    return pl.pallas_call(
        functools.partial(cross_kernel, group, joint, mode),
        out_shape=[dq_shape] + [jax.ShapeDtypeStruct(kvs[0].shape, jnp.bfloat16)] * len(kvs),
        grid_spec=pltpu.PrefetchScalarGridSpec(
            num_scalar_prefetch=1,
            grid=(count,),
            in_specs=in_specs,
            out_specs=[big if final else part] + [pair] * len(kvs),
            scratch_shapes=[pltpu.VMEM((most * rows, group * rows), jnp.bfloat16)] * 2
            + [pltpu.VMEM((most * rows, HEAD_SIZE), jnp.bfloat16)] * 2
            + ([pltpu.VMEM((rows, wide), jnp.float32)] if final else []),
        ),
        input_output_aliases=aliases,
        compiler_params=params(),
        cost_estimate=pl.CostEstimate(
            flops=20 * count * group * rows * rows * HEAD_SIZE * len(kvs),
            bytes_accessed=rows * count * wide * 12,
            transcendentals=0,
        ),
        name="cross",
    )(*args)


def finish_kernel(sizes, parts, c_ref, s_ref, *refs):
    refs = list(refs)
    dk_ref, dv_ref = refs[-2:]
    c, s = c_ref[...], s_ref[...]
    g = 0
    for size in sizes:
        in_refs = [refs.pop(0) for _ in range(parts)]
        for i in range(size):
            a, b = g * HEAD_SIZE, 2 * i * HEAD_SIZE
            total = in_refs[0][:, b : b + 2 * HEAD_SIZE]
            for ref in in_refs[1:]:
                total = total + ref[:, b : b + 2 * HEAD_SIZE].astype(jnp.float32)
            gk = total[:, :HEAD_SIZE]
            dk_ref[:, a : a + HEAD_SIZE] = turn_back(gk, c, s).astype(jnp.bfloat16)
            dv_ref[:, a : a + HEAD_SIZE] = total[:, HEAD_SIZE:].astype(jnp.bfloat16)
            g += 1


def finish(sizes, chunks, c, s):
    rows = chunks[0][0].shape[0]
    width = sum(sizes) * HEAD_SIZE
    return pl.pallas_call(
        functools.partial(finish_kernel, sizes, len(chunks[0])),
        out_shape=[jax.ShapeDtypeStruct((rows, width), jnp.bfloat16)] * 2,
        compiler_params=params(0),
        name="finish",
    )(c, s, *[x for chunk in chunks for x in chunk])


def body(
    queries,
    unrotated_keys,
    value_rows,
    outputs,
    output_gradient,
    saved_logsumexp,
    ancestors,
    placement,
    positions,
):
    hops = lax.axis_size("head")
    places = lax.axis_size("ctx")
    here = lax.axis_index("ctx")
    me = lax.axis_index("head")
    rows = queries.shape[0]
    assert rows * hops == TREE_BLOCK and placement.shape[0] == places
    c, s = rope_tables(positions)

    match = ancestors[placement][:, :1] == placement[None, :]
    source = jnp.argmax(match, axis=1).astype(jnp.int32)
    present = jnp.any(match, axis=1).astype(jnp.int32)

    kv_count = unrotated_keys.shape[1] // HEAD_SIZE
    sizes = split(kv_count)
    chunks = range(len(sizes))
    firsts = [sum(sizes[:g]) for g in chunks]

    def exchange(x):
        width = x.shape[-1]
        return lax.all_to_all(
            x.reshape(places, rows // places, width), "ctx", 0, 0, tiled=True
        )

    def shift(x, n, wrap):
        route = [(i, (i + n) % hops) for i in range(hops) if wrap or 0 <= i + n < hops]
        return lax.ppermute(x, "head", route)

    kv = pack(sizes, unrotated_keys, value_rows, c, s)
    own_flags = jnp.stack([(me >= n).astype(jnp.int32) for n in range(1, hops)])
    parent_flag = present[here][None]
    own_sets, parent_sets = (1,) * (hops - 1), (hops,)

    grad_queries = None
    own_dkv, children, fetched = [], [], []
    for g in chunks:
        send = kv[g]
        if g:
            send, fetched[g - 1] = lax.optimization_barrier((send, fetched[g - 1]))
        middle = exchange(send)
        picked = pick(source, middle)
        fetched.append(exchange(picked))
    for g in chunks:
        own_kv = [shift(kv[g], n, False) for n in range(1, hops)]
        rq, delta, dq, local = diagonal(
            firsts[g], sizes[g], kv_count, queries, output_gradient, outputs,
            saved_logsumexp, c, s, kv[g],
        )
        near = fetched[g].reshape(rows, -1)
        parent_kv = [near] + [shift(near, n, True) for n in range(1, hops)]
        dq, *own_part = cross(
            firsts[g], sizes[g], kv_count, own_flags, own_sets, rq, output_gradient,
            saved_logsumexp, delta, c, s, dq, own_kv,
        )
        back = [shift(own_part[n - 1], -n, False) for n in range(1, hops)]
        own_dkv.append([local] + back)
        grad_queries, *part = cross(
            firsts[g], sizes[g], kv_count, parent_flag, parent_sets, rq, output_gradient,
            saved_logsumexp, delta, c, s, dq, parent_kv, grad_queries, True,
        )
        far_part = [shift(part[n], -n, True) for n in range(1, hops)]
        total = part[0].astype(jnp.float32)
        for x in far_part:
            total = total + x.astype(jnp.float32)
        send = total.astype(jnp.bfloat16)
        if g:
            send, children[g - 1] = lax.optimization_barrier((send, children[g - 1]))
        else:
            send, fetched[-1] = lax.optimization_barrier((send, fetched[-1]))
        up = exchange(send)
        merged = merge(source, present, up)
        children.append(exchange(merged))
    grad_keys, grad_values = finish(
        sizes, [own_dkv[g] + [children[g].reshape(rows, -1)] for g in chunks], c, s
    )
    return (grad_queries, grad_keys, grad_values)


def split(kv_count):
    return (kv_count // 2, kv_count - kv_count // 2)


def solution(mesh):
    return jax.shard_map(
        body,
        mesh=mesh,
        in_specs=(
            P(("ctx", "head"), None),
            P(("ctx", "head"), None),
            P(("ctx", "head"), None),
            P(("ctx", "head"), None),
            P(("ctx", "head"), None),
            P(None, ("ctx", "head")),
            P(),
            P(),
            P(("ctx", "head")),
        ),
        out_specs=(P(("ctx", "head"), None), P(("ctx", "head"), None), P(("ctx", "head"), None)),
        check_vma=False,
    )
```

```python
import functools
import math

import jax
import jax.numpy as jnp
from jax import lax
from jax.experimental import pallas as pl
from jax.experimental.pallas import tpu as pltpu
from jax.sharding import PartitionSpec as P


HEAD_SIZE = 128
TREE_BLOCK = 512
LOG2E = math.log2(math.e)
LN2 = math.log(2.0)
SCALE = 1.0 / math.sqrt(HEAD_SIZE)
rope_base = 500000.0
VMEM_LIMIT = 60 * 1024 * 1024
NT = (((1,), (1,)), ((), ()))
NN = (((1,), (0,)), ((), ()))
TN = (((0,), (0,)), ((), ()))


def rope_tables(positions):
    half_dim = HEAD_SIZE // 2
    freq_index = jnp.arange(half_dim, dtype=jnp.float32)
    inverse = rope_base ** (-(2.0 * freq_index / HEAD_SIZE))
    angles = positions.astype(jnp.float32)[:, None] * inverse[None, :]
    c, s = jnp.cos(angles), jnp.sin(angles)
    return jnp.concatenate([c, c], -1), jnp.concatenate([-s, s], -1)


def dot(a, b, dims):
    return lax.dot_general(a, b, dims, preferred_element_type=jnp.float32)


def turn(x, c, s):
    return x * c + pltpu.roll(x, HEAD_SIZE // 2, 1) * s


def turn_back(x, c, s):
    return x * c - pltpu.roll(x, HEAD_SIZE // 2, 1) * s


def params(n=1):
    return pltpu.CompilerParams(
        dimension_semantics=("arbitrary",) * n, vmem_limit_bytes=VMEM_LIMIT
    )


def pack_kernel(k_ref, v_ref, c_ref, s_ref, o_ref):
    c, s = c_ref[...], s_ref[...]
    for g in range(k_ref.shape[1] // HEAD_SIZE):
        a, b = g * HEAD_SIZE, 2 * g * HEAD_SIZE
        x = k_ref[:, a : a + HEAD_SIZE].astype(jnp.float32)
        o_ref[:, b : b + HEAD_SIZE] = turn(x, c, s).astype(jnp.bfloat16)
        o_ref[:, b + HEAD_SIZE : b + 2 * HEAD_SIZE] = v_ref[:, a : a + HEAD_SIZE]


def pack(keys, values, c, s):
    rows, width = keys.shape
    return pl.pallas_call(
        pack_kernel,
        out_shape=jax.ShapeDtypeStruct((rows, 2 * width), jnp.bfloat16),
        compiler_params=params(0),
        name="pack",
    )(keys, values, c, s)


def pick_kernel(source_ref, x_ref, o_ref):
    for d in range(x_ref.shape[0]):
        o_ref[d] = x_ref[source_ref[d]]


def pick(source, x):
    return pl.pallas_call(
        pick_kernel,
        out_shape=jax.ShapeDtypeStruct(x.shape, x.dtype),
        in_specs=[
            pl.BlockSpec(memory_space=pltpu.SMEM),
            pl.BlockSpec(memory_space=pltpu.VMEM),
        ],
        out_specs=pl.BlockSpec(memory_space=pltpu.VMEM),
        compiler_params=params(0),
        name="pick",
    )(source, x)


def merge_kernel(source_ref, present_ref, *refs):
    *x_refs, o_ref, acc_ref = refs
    acc_ref[...] = jnp.zeros_like(acc_ref)
    for d in range(o_ref.shape[0]):

        @pl.when(present_ref[d] != 0)
        def _():
            at = 0
            for x_ref in x_refs:
                width = x_ref.shape[2]
                acc_ref[source_ref[d], :, at : at + width] += x_ref[d].astype(jnp.float32)
                at += width

    o_ref[...] = acc_ref[...].astype(o_ref.dtype)


def merge(source, present, xs):
    shape = xs[0].shape[:2] + (sum(x.shape[2] for x in xs),)
    return pl.pallas_call(
        merge_kernel,
        out_shape=jax.ShapeDtypeStruct(shape, xs[0].dtype),
        in_specs=[pl.BlockSpec(memory_space=pltpu.SMEM)] * 2
        + [pl.BlockSpec(memory_space=pltpu.VMEM)] * len(xs),
        out_specs=pl.BlockSpec(memory_space=pltpu.VMEM),
        scratch_shapes=[pltpu.VMEM(shape, jnp.float32)],
        compiler_params=params(0),
        name="merge",
    )(source, present, *xs)


def fronts(rq, do, lse, delta, k, v, mask=None):
    prob = jnp.exp2(dot(k, rq, NT) - lse)
    if mask is not None:
        prob = jnp.where(mask, prob, 0.0)
    grad_score = prob * (dot(v, do, NT) - delta)
    return prob.astype(jnp.bfloat16), grad_score.astype(jnp.bfloat16)


def stacked(ref, group):
    return jnp.concatenate([ref[:, cols_of(h)] for h in range(group)], 0)


def heads_of(width, kv_count):
    return width // HEAD_SIZE // kv_count


def cols_of(h):
    return slice(h * HEAD_SIZE, (h + 1) * HEAD_SIZE)


def diagonal_kernel(group, q_ref, do_ref, out_ref, lse_ref, c_ref, s_ref, kv_ref, rq_ref, delta_ref, dq_ref, dkv_ref, p_ref, ds_ref):
    rows = q_ref.shape[0]
    c, s = c_ref[...] * (SCALE * LOG2E), s_ref[...] * (SCALE * LOG2E)
    key_at = lax.broadcasted_iota(jnp.int32, (rows, rows), 0)
    query_at = lax.broadcasted_iota(jnp.int32, (rows, rows), 1)
    causal = key_at <= query_at
    k = kv_ref[:, :HEAD_SIZE]
    v = kv_ref[:, HEAD_SIZE:]
    for h in range(group):
        cols, lanes = cols_of(h), slice(h * rows, (h + 1) * rows)
        do = do_ref[:, cols]
        rq = turn(q_ref[:, cols].astype(jnp.float32), c, s).astype(jnp.bfloat16)
        rq_ref[:, cols] = rq
        product = do.astype(jnp.float32) * out_ref[:, cols].astype(jnp.float32)
        delta = jnp.sum(product.T, axis=0, keepdims=True)
        delta_ref[h : h + 1, :] = delta
        p_ref[:, lanes], ds_ref[:, lanes] = fronts(
            rq, do, lse_ref[h : h + 1, :] * LOG2E, delta, k, v, causal
        )
    dkv_ref[:, :HEAD_SIZE] = dot(ds_ref[...], stacked(rq_ref, group), NN) * LN2
    dkv_ref[:, HEAD_SIZE:] = dot(p_ref[...], stacked(do_ref, group), NN)
    for h in range(group):
        dq_ref[:, cols_of(h)] = dot(ds_ref[:, h * rows : (h + 1) * rows], k, TN)


def diagonal(q, do, out, lse, c, s, kv):
    rows, width = q.shape
    kv_count = count = kv.shape[1] // (2 * HEAD_SIZE)
    first = 0
    group = heads_of(width, kv_count)
    wide = group * HEAD_SIZE
    big = pl.BlockSpec((rows, wide), lambda g: (0, g + first))
    row = pl.BlockSpec((group, rows), lambda g: (g + first, 0))
    table = pl.BlockSpec((rows, HEAD_SIZE), lambda g: (0, 0))
    pair = pl.BlockSpec((rows, 2 * HEAD_SIZE), lambda g: (0, g))
    part = pl.BlockSpec((rows, wide), lambda g: (0, g))
    part_row = pl.BlockSpec((group, rows), lambda g: (g, 0))
    return pl.pallas_call(
        functools.partial(diagonal_kernel, group),
        out_shape=[
            jax.ShapeDtypeStruct((rows, count * wide), jnp.bfloat16),
            jax.ShapeDtypeStruct((count * group, rows), jnp.float32),
            jax.ShapeDtypeStruct((rows, count * wide), jnp.float32),
            jax.ShapeDtypeStruct((rows, count * 2 * HEAD_SIZE), jnp.float32),
        ],
        grid=(count,),
        in_specs=[big, big, big, row, table, table, pair],
        out_specs=[part, part_row, part, pair],
        scratch_shapes=[pltpu.VMEM((rows, group * rows), jnp.bfloat16)] * 2,
        compiler_params=params(),
        cost_estimate=pl.CostEstimate(
            flops=20 * count * group * rows * rows * HEAD_SIZE,
            bytes_accessed=rows * count * wide * 12,
            transcendentals=0,
        ),
        name="diagonal",
    )(q, do, out, lse, c, s, kv)


def cross_kernel(group, joint, final, flag_ref, rq_ref, do_ref, lse_ref, delta_ref, c_ref, s_ref, dq_in_ref, *refs):
    sets = len(joint)
    refs = list(refs)
    kv_refs = [refs.pop(0) for _ in range(sum(joint))]
    if final == 2:
        refs.pop(0)
    dq_ref = refs.pop(0)
    dkv_refs = [refs.pop(0) for _ in range(sum(joint))]
    p_ref, ds_ref, k_ref, v_ref = refs[:4]
    total_ref = refs[4] if final else dq_ref
    rows = rq_ref.shape[0]
    c, s = c_ref[...] * SCALE, s_ref[...] * SCALE

    def put(cols, total):
        if final and sets == 1:
            dq_ref[:, cols] = turn_back(total, c, s).astype(jnp.bfloat16)
        else:
            total_ref[:, cols] = total

    def run(members, fresh):
        here = slice(0, len(members) * rows)
        for n, m in enumerate(members):
            k_ref[n * rows : (n + 1) * rows] = kv_refs[m][:, :HEAD_SIZE]
            v_ref[n * rows : (n + 1) * rows] = kv_refs[m][:, HEAD_SIZE:]
        k = k_ref[here]
        for h in range(group):
            lanes = slice(h * rows, (h + 1) * rows)
            p_ref[here, lanes], ds_ref[here, lanes] = fronts(
                rq_ref[:, cols_of(h)],
                do_ref[:, cols_of(h)],
                lse_ref[h : h + 1, :] * LOG2E,
                delta_ref[h : h + 1, :],
                k,
                v_ref[here],
            )
        gk = dot(ds_ref[here], stacked(rq_ref, group), NN) * LN2
        gv = dot(p_ref[here], stacked(do_ref, group), NN)
        for n, m in enumerate(members):
            own = slice(n * rows, (n + 1) * rows)
            dkv_refs[m][:, :HEAD_SIZE] = gk[own].astype(jnp.bfloat16)
            dkv_refs[m][:, HEAD_SIZE:] = gv[own].astype(jnp.bfloat16)
        for h in range(group):
            cols = cols_of(h)
            before = dq_in_ref[:, cols] if fresh else total_ref[:, cols]
            put(cols, before + dot(ds_ref[here, h * rows : (h + 1) * rows], k, TN))

    def skip(members, fresh):
        if fresh:
            for h in range(group):
                put(cols_of(h), dq_in_ref[:, cols_of(h)])
        for m in members:
            dkv_refs[m][...] = jnp.zeros_like(dkv_refs[m])

    start = 0
    for i, size in enumerate(joint):
        members = tuple(range(start, start + size))
        start += size
        pl.when(flag_ref[i] != 0)(functools.partial(run, members, i == 0))
        pl.when(flag_ref[i] == 0)(functools.partial(skip, members, i == 0))
    if final and sets > 1:
        for h in range(group):
            cols = cols_of(h)
            dq_ref[:, cols] = turn_back(total_ref[:, cols], c, s).astype(jnp.bfloat16)


def cross(first, count, flags, joint, rq, do, lse, delta, c, s, dq, kvs, whole=None, final=False):
    rows, width = do.shape
    kv_count = kvs[0].shape[1] // (2 * HEAD_SIZE)
    group = heads_of(width, kv_count)
    wide = group * HEAD_SIZE
    most = max(joint)
    big = pl.BlockSpec((rows, wide), lambda g, i: (0, g + first))
    row = pl.BlockSpec((group, rows), lambda g, i: (g + first, 0))
    table = pl.BlockSpec((rows, HEAD_SIZE), lambda g, i: (0, 0))
    pair = pl.BlockSpec((rows, 2 * HEAD_SIZE), lambda g, i: (0, g))
    shifted = pl.BlockSpec((rows, 2 * HEAD_SIZE), lambda g, i: (0, g + first))
    args = [flags, rq, do, lse, delta, c, s, dq, *kvs]
    in_specs = [big, big, row, row, table, table, big]
    in_specs += [shifted if x.shape == kvs[0].shape else pair for x in kvs]
    mode = 0
    aliases = {}
    if final:
        mode = 1
        if whole is not None:
            mode = 2
            aliases = {len(args): 0}
            args.append(whole)
            in_specs.append(pl.BlockSpec(memory_space=pl.ANY))
    dq_shape = (
        jax.ShapeDtypeStruct((rows, width), jnp.bfloat16)
        if final
        else jax.ShapeDtypeStruct(dq.shape, jnp.float32)
    )
    return pl.pallas_call(
        functools.partial(cross_kernel, group, joint, mode),
        out_shape=[dq_shape]
        + [jax.ShapeDtypeStruct((rows, count * 2 * HEAD_SIZE), jnp.bfloat16)] * len(kvs),
        grid_spec=pltpu.PrefetchScalarGridSpec(
            num_scalar_prefetch=1,
            grid=(count,),
            in_specs=in_specs,
            out_specs=[big] + [pair] * len(kvs),
            scratch_shapes=[pltpu.VMEM((most * rows, group * rows), jnp.bfloat16)] * 2
            + [pltpu.VMEM((most * rows, HEAD_SIZE), jnp.bfloat16)] * 2
            + ([pltpu.VMEM((rows, wide), jnp.float32)] if final else []),
        ),
        input_output_aliases=aliases,
        compiler_params=params(),
        cost_estimate=pl.CostEstimate(
            flops=20 * count * group * rows * rows * HEAD_SIZE * len(kvs),
            bytes_accessed=rows * count * wide * 12,
            transcendentals=0,
        ),
        name="cross",
    )(*args)


def finish_kernel(parts, own_ref, c_ref, s_ref, *refs):
    in_refs = refs[:parts]
    dk_ref, dv_ref = refs[parts:]
    c, s = c_ref[...], s_ref[...]
    for g in range(dk_ref.shape[1] // HEAD_SIZE):
        a, b = g * HEAD_SIZE, 2 * g * HEAD_SIZE
        total = own_ref[:, b : b + 2 * HEAD_SIZE]
        for ref in in_refs:
            total = total + ref[:, b : b + 2 * HEAD_SIZE].astype(jnp.float32)
        gk = total[:, :HEAD_SIZE]
        dk_ref[:, a : a + HEAD_SIZE] = turn_back(gk, c, s).astype(jnp.bfloat16)
        dv_ref[:, a : a + HEAD_SIZE] = total[:, HEAD_SIZE:].astype(jnp.bfloat16)


def finish(local, parts, c, s):
    rows, width = local.shape
    return pl.pallas_call(
        functools.partial(finish_kernel, len(parts)),
        out_shape=[jax.ShapeDtypeStruct((rows, width // 2), jnp.bfloat16)] * 2,
        compiler_params=params(0),
        name="finish",
    )(local, c, s, *parts)


def body(
    queries,
    unrotated_keys,
    value_rows,
    outputs,
    output_gradient,
    saved_logsumexp,
    ancestors,
    placement,
    positions,
):
    hops = lax.axis_size("head")
    places = lax.axis_size("ctx")
    here = lax.axis_index("ctx")
    me = lax.axis_index("head")
    rows = queries.shape[0]
    assert rows * hops == TREE_BLOCK and placement.shape[0] == places
    c, s = rope_tables(positions)

    match = ancestors[placement][:, :1] == placement[None, :]
    source = jnp.argmax(match, axis=1).astype(jnp.int32)
    present = jnp.any(match, axis=1).astype(jnp.int32)

    sizes = split(unrotated_keys.shape[1] // HEAD_SIZE)
    chunks = range(len(sizes))
    firsts = [sum(sizes[:g]) for g in chunks]

    def exchange(x):
        width = x.shape[-1]
        return lax.all_to_all(
            x.reshape(places, rows // places, width), "ctx", 0, 0, tiled=True
        )

    def shift(x, n, wrap):
        route = [(i, (i + n) % hops) for i in range(hops) if wrap or 0 <= i + n < hops]
        return lax.ppermute(x, "head", route)

    kv = pack(unrotated_keys, value_rows, c, s)
    own_flags = jnp.stack([(me >= n).astype(jnp.int32) for n in range(1, hops)])
    parent_flag = present[here][None]
    own_sets, parent_sets = (1,) * (hops - 1), (hops,)

    middle = exchange(kv)
    own_kv = [shift(kv, n, False) for n in range(1, hops)]
    rq, delta, dq, local = diagonal(
        queries, output_gradient, outputs, saved_logsumexp, c, s, kv
    )
    picked = pick(source, middle)
    near = exchange(picked).reshape(rows, -1)
    dq, *own_part = cross(
        0, sum(sizes), own_flags, own_sets, rq, output_gradient,
        saved_logsumexp, delta, c, s, dq, own_kv,
    )
    back = [shift(own_part[n - 1], -n, False) for n in range(1, hops)]
    grad_queries = None
    ups = []
    for g in chunks:
        at = 2 * HEAD_SIZE * firsts[g]
        piece = near[:, at : at + 2 * HEAD_SIZE * sizes[g]]
        parent_kv = [near] + [shift(piece, n, True) for n in range(1, hops)]
        grad_queries, *part = cross(
            firsts[g], sizes[g], parent_flag, parent_sets, rq, output_gradient,
            saved_logsumexp, delta, c, s, dq, parent_kv, grad_queries, True,
        )
        far_part = [shift(part[n], -n, True) for n in range(1, hops)]
        total = part[0].astype(jnp.float32)
        for x in far_part:
            total = total + x.astype(jnp.float32)
        send = total.astype(jnp.bfloat16)
        if g:
            send, ups[-1] = lax.optimization_barrier((send, ups[-1]))
        ups.append(exchange(send))
    merged = merge(source, present, ups)
    children = exchange(merged).reshape(rows, -1)
    grad_keys, grad_values = finish(local, back + [children], c, s)
    return (grad_queries, grad_keys, grad_values)


def split(kv_count):
    first = kv_count // 4
    second = (kv_count - first) // 2
    return (first, second, kv_count - first - second)


def solution(mesh):
    return jax.shard_map(
        body,
        mesh=mesh,
        in_specs=(
            P(("ctx", "head"), None),
            P(("ctx", "head"), None),
            P(("ctx", "head"), None),
            P(("ctx", "head"), None),
            P(("ctx", "head"), None),
            P(None, ("ctx", "head")),
            P(),
            P(),
            P(("ctx", "head")),
        ),
        out_specs=(P(("ctx", "head"), None), P(("ctx", "head"), None), P(("ctx", "head"), None)),
        check_vma=False,
    )
```

```python
import functools
import math

import jax
import jax.numpy as jnp
from jax import lax
from jax.experimental import pallas as pl
from jax.experimental.pallas import tpu as pltpu
from jax.sharding import PartitionSpec as P


HEAD_SIZE = 128
TREE_BLOCK = 512
LOG2E = math.log2(math.e)
LN2 = math.log(2.0)
SCALE = 1.0 / math.sqrt(HEAD_SIZE)
rope_base = 500000.0
MIB = 1024 * 1024
NT = (((1,), (1,)), ((), ()))
NN = (((1,), (0,)), ((), ()))
TN = (((0,), (0,)), ((), ()))


def rope_tables(positions):
    half_dim = HEAD_SIZE // 2
    freq_index = jnp.arange(half_dim, dtype=jnp.float32)
    inverse = rope_base ** (-(2.0 * freq_index / HEAD_SIZE))
    angles = positions.astype(jnp.float32)[:, None] * inverse[None, :]
    c, s = jnp.cos(angles), jnp.sin(angles)
    return jnp.concatenate([c, c], -1), jnp.concatenate([-s, s], -1)


def dot(a, b, dims):
    return lax.dot_general(a, b, dims, preferred_element_type=jnp.float32)


def turn(x, c, s):
    return x * c + pltpu.roll(x, HEAD_SIZE // 2, 1) * s


def turn_back(x, c, s):
    return x * c - pltpu.roll(x, HEAD_SIZE // 2, 1) * s


def params(n, mib):
    return pltpu.CompilerParams(
        dimension_semantics=("arbitrary",) * n, vmem_limit_bytes=mib * MIB
    )


def pair_kernel(k_ref, v_ref, o_ref):
    for g in range(k_ref.shape[1] // HEAD_SIZE):
        a, b = g * HEAD_SIZE, 2 * g * HEAD_SIZE
        o_ref[:, b : b + HEAD_SIZE] = k_ref[:, a : a + HEAD_SIZE]
        o_ref[:, b + HEAD_SIZE : b + 2 * HEAD_SIZE] = v_ref[:, a : a + HEAD_SIZE]


def turn_keys_kernel(x_ref, c_ref, s_ref, o_ref):
    c, s = c_ref[...], s_ref[...]
    for b in range(0, x_ref.shape[1], 2 * HEAD_SIZE):
        k, v = slice(b, b + HEAD_SIZE), slice(b + HEAD_SIZE, b + 2 * HEAD_SIZE)
        o_ref[:, k] = turn(x_ref[:, k].astype(jnp.float32), c, s).astype(jnp.bfloat16)
        o_ref[:, v] = x_ref[:, v]


def pair(keys, values):
    rows, width = keys.shape
    return pl.pallas_call(
        pair_kernel,
        out_shape=jax.ShapeDtypeStruct((rows, 2 * width), jnp.bfloat16),
        compiler_params=params(0, 6),
        name="pair",
    )(keys, values)


def turn_keys(x, c, s):
    return pl.pallas_call(
        turn_keys_kernel,
        out_shape=jax.ShapeDtypeStruct(x.shape, x.dtype),
        compiler_params=params(0, 6),
        name="turn_keys",
    )(x, c, s)


def pick_kernel(source_ref, x_ref, c_ref, s_ref, o_ref):
    for d in range(x_ref.shape[0]):
        at = source_ref[d]
        c, s = c_ref[at], s_ref[at]
        for b in range(0, x_ref.shape[2], 2 * HEAD_SIZE):
            k, v = slice(b, b + HEAD_SIZE), slice(b + HEAD_SIZE, b + 2 * HEAD_SIZE)
            x = x_ref[at, :, k].astype(jnp.float32)
            o_ref[d, :, k] = turn(x, c, s).astype(jnp.bfloat16)
            o_ref[d, :, v] = x_ref[at, :, v]


def pick(source, x, c, s):
    return pl.pallas_call(
        pick_kernel,
        out_shape=jax.ShapeDtypeStruct(x.shape, x.dtype),
        in_specs=[pl.BlockSpec(memory_space=pltpu.SMEM)]
        + [pl.BlockSpec(memory_space=pltpu.VMEM)] * 3,
        out_specs=pl.BlockSpec(memory_space=pltpu.VMEM),
        compiler_params=params(0, 8),
        name="pick",
    )(source, x, c, s)


def merge_kernel(source_ref, present_ref, c_ref, s_ref, *refs):
    *x_refs, o_ref, acc_ref = refs
    acc_ref[...] = jnp.zeros_like(acc_ref)
    for d in range(o_ref.shape[0]):

        @pl.when(present_ref[d] != 0)
        def _():
            at = 0
            for x_ref in x_refs:
                width = x_ref.shape[2]
                acc_ref[source_ref[d], :, at : at + width] += x_ref[d].astype(jnp.float32)
                at += width

    for d in range(o_ref.shape[0]):
        c, s = c_ref[d], s_ref[d]
        for b in range(0, o_ref.shape[2], 2 * HEAD_SIZE):
            k, v = slice(b, b + HEAD_SIZE), slice(b + HEAD_SIZE, b + 2 * HEAD_SIZE)
            o_ref[d, :, k] = turn_back(acc_ref[d, :, k], c, s).astype(o_ref.dtype)
            o_ref[d, :, v] = acc_ref[d, :, v].astype(o_ref.dtype)


def merge(source, present, c, s, xs):
    shape = xs[0].shape[:2] + (sum(x.shape[2] for x in xs),)
    return pl.pallas_call(
        merge_kernel,
        out_shape=jax.ShapeDtypeStruct(shape, xs[0].dtype),
        in_specs=[pl.BlockSpec(memory_space=pltpu.SMEM)] * 2
        + [pl.BlockSpec(memory_space=pltpu.VMEM)] * (2 + len(xs)),
        out_specs=pl.BlockSpec(memory_space=pltpu.VMEM),
        scratch_shapes=[pltpu.VMEM(shape, jnp.float32)],
        compiler_params=params(0, 10),
        name="merge",
    )(source, present, c, s, *xs)


def fronts(rq, do, lse, delta, k, v, mask=None):
    prob = jnp.exp2(dot(k, rq, NT) - lse)
    if mask is not None:
        prob = jnp.where(mask, prob, 0.0)
    grad_score = prob * (dot(v, do, NT) - delta)
    return prob.astype(jnp.bfloat16), grad_score.astype(jnp.bfloat16)


def stacked(ref, group):
    return jnp.concatenate([ref[:, cols_of(h)] for h in range(group)], 0)


def heads_of(width, kv_count):
    return width // HEAD_SIZE // kv_count


def cols_of(h):
    return slice(h * HEAD_SIZE, (h + 1) * HEAD_SIZE)


def diagonal_kernel(group, q_ref, do_ref, out_ref, lse_ref, c_ref, s_ref, kv_ref, rq_ref, delta_ref, dq_ref, dkv_ref, p_ref, ds_ref):
    rows = q_ref.shape[0]
    c, s = c_ref[...] * (SCALE * LOG2E), s_ref[...] * (SCALE * LOG2E)
    key_at = lax.broadcasted_iota(jnp.int32, (rows, rows), 0)
    query_at = lax.broadcasted_iota(jnp.int32, (rows, rows), 1)
    causal = key_at <= query_at
    k = kv_ref[:, :HEAD_SIZE]
    v = kv_ref[:, HEAD_SIZE:]
    for h in range(group):
        cols, lanes = cols_of(h), slice(h * rows, (h + 1) * rows)
        do = do_ref[:, cols]
        rq = turn(q_ref[:, cols].astype(jnp.float32), c, s).astype(jnp.bfloat16)
        rq_ref[:, cols] = rq
        product = do.astype(jnp.float32) * out_ref[:, cols].astype(jnp.float32)
        delta = jnp.sum(product.T, axis=0, keepdims=True)
        delta_ref[h : h + 1, :] = delta
        p_ref[:, lanes], ds_ref[:, lanes] = fronts(
            rq, do, lse_ref[h : h + 1, :] * LOG2E, delta, k, v, causal
        )
    dkv_ref[:, :HEAD_SIZE] = dot(ds_ref[...], stacked(rq_ref, group), NN) * LN2
    dkv_ref[:, HEAD_SIZE:] = dot(p_ref[...], stacked(do_ref, group), NN)
    for h in range(group):
        dq_ref[:, cols_of(h)] = dot(ds_ref[:, h * rows : (h + 1) * rows], k, TN)


def diagonal(q, do, out, lse, c, s, kv):
    rows, width = q.shape
    kv_count = count = kv.shape[1] // (2 * HEAD_SIZE)
    first = 0
    group = heads_of(width, kv_count)
    wide = group * HEAD_SIZE
    big = pl.BlockSpec((rows, wide), lambda g: (0, g + first))
    row = pl.BlockSpec((group, rows), lambda g: (g + first, 0))
    table = pl.BlockSpec((rows, HEAD_SIZE), lambda g: (0, 0))
    pair = pl.BlockSpec((rows, 2 * HEAD_SIZE), lambda g: (0, g))
    part = pl.BlockSpec((rows, wide), lambda g: (0, g))
    part_row = pl.BlockSpec((group, rows), lambda g: (g, 0))
    return pl.pallas_call(
        functools.partial(diagonal_kernel, group),
        out_shape=[
            jax.ShapeDtypeStruct((rows, count * wide), jnp.bfloat16),
            jax.ShapeDtypeStruct((count * group, rows), jnp.float32),
            jax.ShapeDtypeStruct((rows, count * wide), jnp.float32),
            jax.ShapeDtypeStruct((rows, count * 2 * HEAD_SIZE), jnp.float32),
        ],
        grid=(count,),
        in_specs=[big, big, big, row, table, table, pair],
        out_specs=[part, part_row, part, pair],
        scratch_shapes=[pltpu.VMEM((rows, group * rows), jnp.bfloat16)] * 2,
        compiler_params=params(1, 24),
        cost_estimate=pl.CostEstimate(
            flops=20 * count * group * rows * rows * HEAD_SIZE,
            bytes_accessed=rows * count * wide * 12,
            transcendentals=0,
        ),
        name="diagonal",
    )(q, do, out, lse, c, s, kv)


def cross_kernel(group, joint, final, flag_ref, rq_ref, do_ref, lse_ref, delta_ref, c_ref, s_ref, dq_in_ref, *refs):
    sets = len(joint)
    refs = list(refs)
    kv_refs = [refs.pop(0) for _ in range(sum(joint))]
    if final == 2:
        refs.pop(0)
    dq_ref = refs.pop(0)
    dkv_refs = [refs.pop(0) for _ in range(sum(joint))]
    p_ref, ds_ref, k_ref, v_ref = refs[:4]
    total_ref = refs[4] if final else dq_ref
    rows = rq_ref.shape[0]
    c, s = c_ref[...] * SCALE, s_ref[...] * SCALE

    def put(cols, total):
        if final and sets == 1:
            dq_ref[:, cols] = turn_back(total, c, s).astype(jnp.bfloat16)
        else:
            total_ref[:, cols] = total

    def run(members, fresh):
        here = slice(0, len(members) * rows)
        for n, m in enumerate(members):
            k_ref[n * rows : (n + 1) * rows] = kv_refs[m][:, :HEAD_SIZE]
            v_ref[n * rows : (n + 1) * rows] = kv_refs[m][:, HEAD_SIZE:]
        k = k_ref[here]
        for h in range(group):
            lanes = slice(h * rows, (h + 1) * rows)
            p_ref[here, lanes], ds_ref[here, lanes] = fronts(
                rq_ref[:, cols_of(h)],
                do_ref[:, cols_of(h)],
                lse_ref[h : h + 1, :] * LOG2E,
                delta_ref[h : h + 1, :],
                k,
                v_ref[here],
            )
        gk = dot(ds_ref[here], stacked(rq_ref, group), NN) * LN2
        gv = dot(p_ref[here], stacked(do_ref, group), NN)
        for n, m in enumerate(members):
            own = slice(n * rows, (n + 1) * rows)
            dkv_refs[m][:, :HEAD_SIZE] = gk[own].astype(jnp.bfloat16)
            dkv_refs[m][:, HEAD_SIZE:] = gv[own].astype(jnp.bfloat16)
        for h in range(group):
            cols = cols_of(h)
            before = dq_in_ref[:, cols] if fresh else total_ref[:, cols]
            put(cols, before + dot(ds_ref[here, h * rows : (h + 1) * rows], k, TN))

    def skip(members, fresh):
        if fresh:
            for h in range(group):
                put(cols_of(h), dq_in_ref[:, cols_of(h)])
        for m in members:
            dkv_refs[m][...] = jnp.zeros_like(dkv_refs[m])

    start = 0
    for i, size in enumerate(joint):
        members = tuple(range(start, start + size))
        start += size
        pl.when(flag_ref[i] != 0)(functools.partial(run, members, i == 0))
        pl.when(flag_ref[i] == 0)(functools.partial(skip, members, i == 0))
    if final and sets > 1:
        for h in range(group):
            cols = cols_of(h)
            dq_ref[:, cols] = turn_back(total_ref[:, cols], c, s).astype(jnp.bfloat16)


def cross(kv_count, first, count, flags, joint, rq, do, lse, delta, c, s, dq, kvs, whole=None, final=False):
    rows, width = do.shape
    group = heads_of(width, kv_count)
    wide = group * HEAD_SIZE
    most = max(joint)
    big = pl.BlockSpec((rows, wide), lambda g, i: (0, g + first))
    row = pl.BlockSpec((group, rows), lambda g, i: (g + first, 0))
    table = pl.BlockSpec((rows, HEAD_SIZE), lambda g, i: (0, 0))
    pair = pl.BlockSpec((rows, 2 * HEAD_SIZE), lambda g, i: (0, g))
    shifted = pl.BlockSpec((rows, 2 * HEAD_SIZE), lambda g, i: (0, g + first))
    args = [flags, rq, do, lse, delta, c, s, dq, *kvs]
    in_specs = [big, big, row, row, table, table, big]
    chunk_width = count * 2 * HEAD_SIZE
    in_specs += [pair if x.shape[1] == chunk_width else shifted for x in kvs]
    mode = 0
    aliases = {}
    if final:
        mode = 1
        if whole is not None:
            mode = 2
            aliases = {len(args): 0}
            args.append(whole)
            in_specs.append(pl.BlockSpec(memory_space=pl.ANY))
    dq_shape = (
        jax.ShapeDtypeStruct((rows, width), jnp.bfloat16)
        if final
        else jax.ShapeDtypeStruct(dq.shape, jnp.float32)
    )
    return pl.pallas_call(
        functools.partial(cross_kernel, group, joint, mode),
        out_shape=[dq_shape]
        + [jax.ShapeDtypeStruct((rows, count * 2 * HEAD_SIZE), jnp.bfloat16)] * len(kvs),
        grid_spec=pltpu.PrefetchScalarGridSpec(
            num_scalar_prefetch=1,
            grid=(count,),
            in_specs=in_specs,
            out_specs=[big] + [pair] * len(kvs),
            scratch_shapes=[pltpu.VMEM((most * rows, group * rows), jnp.bfloat16)] * 2
            + [pltpu.VMEM((most * rows, HEAD_SIZE), jnp.bfloat16)] * 2
            + ([pltpu.VMEM((rows, wide), jnp.float32)] if final else []),
        ),
        input_output_aliases=aliases,
        compiler_params=params(1, 24),
        cost_estimate=pl.CostEstimate(
            flops=20 * count * group * rows * rows * HEAD_SIZE * len(kvs),
            bytes_accessed=rows * count * wide * 12,
            transcendentals=0,
        ),
        name="cross",
    )(*args)


def settle_kernel(own_ref, c_ref, s_ref, *refs):
    *in_refs, o_ref = refs
    c, s = c_ref[...], s_ref[...]
    for b in range(0, o_ref.shape[1], 2 * HEAD_SIZE):
        k, v = slice(b, b + HEAD_SIZE), slice(b + HEAD_SIZE, b + 2 * HEAD_SIZE)
        gk, gv = own_ref[:, k], own_ref[:, v]
        for ref in in_refs:
            gk = gk + ref[:, k].astype(jnp.float32)
            gv = gv + ref[:, v].astype(jnp.float32)
        o_ref[:, k] = turn_back(gk, c, s)
        o_ref[:, v] = gv


def settle(local, parts, c, s):
    return pl.pallas_call(
        settle_kernel,
        out_shape=jax.ShapeDtypeStruct(local.shape, jnp.float32),
        compiler_params=params(0, 12),
        name="settle",
    )(local, c, s, *parts)


def finish_kernel(own_ref, children_ref, dk_ref, dv_ref):
    for g in range(dk_ref.shape[1] // HEAD_SIZE):
        a, b = g * HEAD_SIZE, 2 * g * HEAD_SIZE
        total = own_ref[:, b : b + 2 * HEAD_SIZE]
        total = total + children_ref[:, b : b + 2 * HEAD_SIZE].astype(jnp.float32)
        dk_ref[:, a : a + HEAD_SIZE] = total[:, :HEAD_SIZE].astype(jnp.bfloat16)
        dv_ref[:, a : a + HEAD_SIZE] = total[:, HEAD_SIZE:].astype(jnp.bfloat16)


def finish(base, children):
    rows, width = base.shape
    return pl.pallas_call(
        finish_kernel,
        out_shape=[jax.ShapeDtypeStruct((rows, width // 2), jnp.bfloat16)] * 2,
        compiler_params=params(0, 8),
        name="finish",
    )(base, children)


def body(
    queries,
    unrotated_keys,
    value_rows,
    outputs,
    output_gradient,
    saved_logsumexp,
    ancestors,
    placement,
    positions,
):
    hops = lax.axis_size("head")
    places = lax.axis_size("ctx")
    here = lax.axis_index("ctx")
    me = lax.axis_index("head")
    rows = queries.shape[0]
    assert rows * hops == TREE_BLOCK and placement.shape[0] == places
    c, s = rope_tables(positions)

    match = ancestors[placement][:, :1] == placement[None, :]
    source = jnp.argmax(match, axis=1).astype(jnp.int32)
    present = jnp.any(match, axis=1).astype(jnp.int32)

    kv_count = unrotated_keys.shape[1] // HEAD_SIZE
    sizes = split(kv_count)
    chunks = range(len(sizes))
    firsts = [sum(sizes[:g]) for g in chunks]

    def exchange(x):
        width = x.shape[-1]
        return lax.all_to_all(
            x.reshape(places, rows // places, width), "ctx", 0, 0, tiled=True
        )

    def shift(x, n, wrap):
        route = [(i, (i + n) % hops) for i in range(hops) if wrap or 0 <= i + n < hops]
        return lax.ppermute(x, "head", route)

    raw = pair(unrotated_keys, value_rows)
    own_flags = jnp.stack([(me >= n).astype(jnp.int32) for n in range(1, hops)])
    parent_flag = present[here][None]

    piece_rows = rows // places
    offset = me * rows + here * piece_rows + jnp.arange(piece_rows, dtype=jnp.int32)
    middle_at = (TREE_BLOCK * placement[:, None] + offset[None, :]).reshape(-1)
    middle_c, middle_s = [
        t.reshape(places, piece_rows, HEAD_SIZE) for t in rope_tables(middle_at)
    ]

    middle = exchange(raw)
    kv = turn_keys(raw, c, s)
    own_kv = [shift(kv, n, False) for n in range(1, hops)]
    rq, delta, dq, local = diagonal(
        queries, output_gradient, outputs, saved_logsumexp, c, s, kv
    )
    picked = pick(source, middle, middle_c, middle_s)
    near = exchange(picked).reshape(rows, -1)
    dq, *own_part = cross(
        kv_count, 0, kv_count, own_flags, (1,) * (hops - 1), rq, output_gradient,
        saved_logsumexp, delta, c, s, dq, own_kv,
    )
    back = [shift(own_part[n - 1], -n, False) for n in range(1, hops)]
    base = settle(local, back, c, s)

    far = []
    for g in chunks:
        at = 2 * HEAD_SIZE * firsts[g]
        piece = near[:, at : at + 2 * HEAD_SIZE * sizes[g]]
        far.append([shift(piece, n, True) for n in range(1, hops)])

    def tiles(g, dq, kvs, whole, final):
        return cross(
            kv_count, firsts[g], sizes[g], parent_flag, (len(kvs),), rq, output_gradient,
            saved_logsumexp, delta, c, s, dq, kvs, whole, final,
        )

    grad_queries = None
    ups = []
    for g in chunks:
        part = dq
        if g == 0:
            part, near_part = tiles(g, part, [near], None, False)
        part, *far_part = tiles(g, part, far[g], grad_queries, g == 0)
        if g:
            part, near_part = tiles(g, part, [near], grad_queries, True)
        grad_queries = part
        joined = [shift(x, -n - 1, True) for n, x in enumerate(far_part)]
        total = near_part.astype(jnp.float32)
        for x in joined:
            total = total + x.astype(jnp.float32)
        send = total.astype(jnp.bfloat16)
        if g:
            send, ups[-1] = lax.optimization_barrier((send, ups[-1]))
        ups.append(exchange(send))
    merged = merge(source, present, middle_c, middle_s, ups)
    children = exchange(merged).reshape(rows, -1)
    grad_keys, grad_values = finish(base, children)
    return (grad_queries, grad_keys, grad_values)


def split(kv_count):
    return (kv_count // 2, kv_count - kv_count // 2)


def solution(mesh):
    return jax.shard_map(
        body,
        mesh=mesh,
        in_specs=(
            P(("ctx", "head"), None),
            P(("ctx", "head"), None),
            P(("ctx", "head"), None),
            P(("ctx", "head"), None),
            P(("ctx", "head"), None),
            P(None, ("ctx", "head")),
            P(),
            P(),
            P(("ctx", "head")),
        ),
        out_specs=(P(("ctx", "head"), None), P(("ctx", "head"), None), P(("ctx", "head"), None)),
        check_vma=False,
    )
```

```python
import functools
import math

import jax
import jax.numpy as jnp
from jax import lax
from jax.experimental import pallas as pl
from jax.experimental.pallas import tpu as pltpu
from jax.sharding import PartitionSpec as P


HEAD_SIZE = 128
TREE_BLOCK = 512
LOG2E = math.log2(math.e)
LN2 = math.log(2.0)
SCALE = 1.0 / math.sqrt(HEAD_SIZE)
rope_base = 500000.0
MIB = 1024 * 1024
NT = (((1,), (1,)), ((), ()))
NN = (((1,), (0,)), ((), ()))
TN = (((0,), (0,)), ((), ()))


def rope_tables(positions):
    half_dim = HEAD_SIZE // 2
    freq_index = jnp.arange(half_dim, dtype=jnp.float32)
    inverse = rope_base ** (-(2.0 * freq_index / HEAD_SIZE))
    angles = positions.astype(jnp.float32)[:, None] * inverse[None, :]
    c, s = jnp.cos(angles), jnp.sin(angles)
    return jnp.concatenate([c, c], -1), jnp.concatenate([-s, s], -1)


def dot(a, b, dims):
    return lax.dot_general(a, b, dims, preferred_element_type=jnp.float32)


def turn(x, c, s):
    return x * c + pltpu.roll(x, HEAD_SIZE // 2, 1) * s


def turn_back(x, c, s):
    return x * c - pltpu.roll(x, HEAD_SIZE // 2, 1) * s


def params(n, mib):
    return pltpu.CompilerParams(
        dimension_semantics=("arbitrary",) * n, vmem_limit_bytes=mib * MIB
    )


def pair_kernel(k_ref, v_ref, o_ref):
    for g in range(k_ref.shape[1] // HEAD_SIZE):
        a, b = g * HEAD_SIZE, 2 * g * HEAD_SIZE
        o_ref[:, b : b + HEAD_SIZE] = k_ref[:, a : a + HEAD_SIZE]
        o_ref[:, b + HEAD_SIZE : b + 2 * HEAD_SIZE] = v_ref[:, a : a + HEAD_SIZE]


def turn_keys_kernel(x_ref, c_ref, s_ref, o_ref):
    c, s = c_ref[...], s_ref[...]
    for b in range(0, x_ref.shape[1], 2 * HEAD_SIZE):
        k, v = slice(b, b + HEAD_SIZE), slice(b + HEAD_SIZE, b + 2 * HEAD_SIZE)
        o_ref[:, k] = turn(x_ref[:, k].astype(jnp.float32), c, s).astype(jnp.bfloat16)
        o_ref[:, v] = x_ref[:, v]


def pair(keys, values):
    rows, width = keys.shape
    return pl.pallas_call(
        pair_kernel,
        out_shape=jax.ShapeDtypeStruct((rows, 2 * width), jnp.bfloat16),
        compiler_params=params(0, 60),
        name="pair",
    )(keys, values)


def turn_keys(x, c, s):
    return pl.pallas_call(
        turn_keys_kernel,
        out_shape=jax.ShapeDtypeStruct(x.shape, x.dtype),
        compiler_params=params(0, 60),
        name="turn_keys",
    )(x, c, s)


def pick_kernel(source_ref, x_ref, c_ref, s_ref, o_ref):
    for d in range(x_ref.shape[0]):
        at = source_ref[d]
        c, s = c_ref[at], s_ref[at]
        for b in range(0, x_ref.shape[2], 2 * HEAD_SIZE):
            k, v = slice(b, b + HEAD_SIZE), slice(b + HEAD_SIZE, b + 2 * HEAD_SIZE)
            x = x_ref[at, :, k].astype(jnp.float32)
            o_ref[d, :, k] = turn(x, c, s).astype(jnp.bfloat16)
            o_ref[d, :, v] = x_ref[at, :, v]


def pick(source, x, c, s):
    return pl.pallas_call(
        pick_kernel,
        out_shape=jax.ShapeDtypeStruct(x.shape, x.dtype),
        in_specs=[pl.BlockSpec(memory_space=pltpu.SMEM)]
        + [pl.BlockSpec(memory_space=pltpu.VMEM)] * 3,
        out_specs=pl.BlockSpec(memory_space=pltpu.VMEM),
        compiler_params=params(0, 8),
        name="pick",
    )(source, x, c, s)


def merge_kernel(source_ref, present_ref, c_ref, s_ref, *refs):
    *x_refs, o_ref, acc_ref = refs
    acc_ref[...] = jnp.zeros_like(acc_ref)
    for d in range(o_ref.shape[0]):

        @pl.when(present_ref[d] != 0)
        def _():
            at = 0
            for x_ref in x_refs:
                width = x_ref.shape[2]
                acc_ref[source_ref[d], :, at : at + width] += x_ref[d].astype(jnp.float32)
                at += width

    for d in range(o_ref.shape[0]):
        c, s = c_ref[d], s_ref[d]
        for b in range(0, o_ref.shape[2], 2 * HEAD_SIZE):
            k, v = slice(b, b + HEAD_SIZE), slice(b + HEAD_SIZE, b + 2 * HEAD_SIZE)
            o_ref[d, :, k] = turn_back(acc_ref[d, :, k], c, s).astype(o_ref.dtype)
            o_ref[d, :, v] = acc_ref[d, :, v].astype(o_ref.dtype)


def merge(source, present, c, s, xs):
    shape = xs[0].shape[:2] + (sum(x.shape[2] for x in xs),)
    return pl.pallas_call(
        merge_kernel,
        out_shape=jax.ShapeDtypeStruct(shape, xs[0].dtype),
        in_specs=[pl.BlockSpec(memory_space=pltpu.SMEM)] * 2
        + [pl.BlockSpec(memory_space=pltpu.VMEM)] * (2 + len(xs)),
        out_specs=pl.BlockSpec(memory_space=pltpu.VMEM),
        scratch_shapes=[pltpu.VMEM(shape, jnp.float32)],
        compiler_params=params(0, 10),
        name="merge",
    )(source, present, c, s, *xs)


def fronts(rq, do, lse, delta, k, v, mask=None):
    prob = jnp.exp2(dot(k, rq, NT) - lse)
    if mask is not None:
        prob = jnp.where(mask, prob, 0.0)
    grad_score = prob * (dot(v, do, NT) - delta)
    return prob.astype(jnp.bfloat16), grad_score.astype(jnp.bfloat16)


def stacked(ref, group):
    return jnp.concatenate([ref[:, cols_of(h)] for h in range(group)], 0)


def heads_of(width, kv_count):
    return width // HEAD_SIZE // kv_count


def cols_of(h):
    return slice(h * HEAD_SIZE, (h + 1) * HEAD_SIZE)


def diagonal_kernel(group, q_ref, do_ref, out_ref, lse_ref, c_ref, s_ref, kv_ref, rq_ref, delta_ref, dq_ref, dkv_ref, p_ref, ds_ref):
    rows = q_ref.shape[0]
    c, s = c_ref[...] * (SCALE * LOG2E), s_ref[...] * (SCALE * LOG2E)
    key_at = lax.broadcasted_iota(jnp.int32, (rows, rows), 0)
    query_at = lax.broadcasted_iota(jnp.int32, (rows, rows), 1)
    causal = key_at <= query_at
    k = kv_ref[:, :HEAD_SIZE]
    v = kv_ref[:, HEAD_SIZE:]
    for h in range(group):
        cols, lanes = cols_of(h), slice(h * rows, (h + 1) * rows)
        do = do_ref[:, cols]
        rq = turn(q_ref[:, cols].astype(jnp.float32), c, s).astype(jnp.bfloat16)
        rq_ref[:, cols] = rq
        product = do.astype(jnp.float32) * out_ref[:, cols].astype(jnp.float32)
        delta = jnp.sum(product.T, axis=0, keepdims=True)
        delta_ref[h : h + 1, :] = delta
        p_ref[:, lanes], ds_ref[:, lanes] = fronts(
            rq, do, lse_ref[h : h + 1, :] * LOG2E, delta, k, v, causal
        )
    dkv_ref[:, :HEAD_SIZE] = dot(ds_ref[...], stacked(rq_ref, group), NN) * LN2
    dkv_ref[:, HEAD_SIZE:] = dot(p_ref[...], stacked(do_ref, group), NN)
    for h in range(group):
        dq_ref[:, cols_of(h)] = dot(ds_ref[:, h * rows : (h + 1) * rows], k, TN)


def diagonal(q, do, out, lse, c, s, kv):
    rows, width = q.shape
    kv_count = count = kv.shape[1] // (2 * HEAD_SIZE)
    first = 0
    group = heads_of(width, kv_count)
    wide = group * HEAD_SIZE
    big = pl.BlockSpec((rows, wide), lambda g: (0, g + first))
    row = pl.BlockSpec((group, rows), lambda g: (g + first, 0))
    table = pl.BlockSpec((rows, HEAD_SIZE), lambda g: (0, 0))
    pair = pl.BlockSpec((rows, 2 * HEAD_SIZE), lambda g: (0, g))
    part = pl.BlockSpec((rows, wide), lambda g: (0, g))
    part_row = pl.BlockSpec((group, rows), lambda g: (g, 0))
    return pl.pallas_call(
        functools.partial(diagonal_kernel, group),
        out_shape=[
            jax.ShapeDtypeStruct((rows, count * wide), jnp.bfloat16),
            jax.ShapeDtypeStruct((count * group, rows), jnp.float32),
            jax.ShapeDtypeStruct((rows, count * wide), jnp.float32),
            jax.ShapeDtypeStruct((rows, count * 2 * HEAD_SIZE), jnp.float32),
        ],
        grid=(count,),
        in_specs=[big, big, big, row, table, table, pair],
        out_specs=[part, part_row, part, pair],
        scratch_shapes=[pltpu.VMEM((rows, group * rows), jnp.bfloat16)] * 2,
        compiler_params=params(1, 60),
        cost_estimate=pl.CostEstimate(
            flops=20 * count * group * rows * rows * HEAD_SIZE,
            bytes_accessed=rows * count * wide * 12,
            transcendentals=0,
        ),
        name="diagonal",
    )(q, do, out, lse, c, s, kv)


def cross_kernel(group, joint, final, flag_ref, rq_ref, do_ref, lse_ref, delta_ref, c_ref, s_ref, dq_in_ref, *refs):
    sets = len(joint)
    refs = list(refs)
    kv_refs = [refs.pop(0) for _ in range(sum(joint))]
    if final == 2:
        refs.pop(0)
    dq_ref = refs.pop(0)
    dkv_refs = [refs.pop(0) for _ in range(sum(joint))]
    p_ref, ds_ref, k_ref, v_ref = refs[:4]
    total_ref = refs[4] if final else dq_ref
    rows = rq_ref.shape[0]
    c, s = c_ref[...] * SCALE, s_ref[...] * SCALE

    def put(cols, total):
        if final and sets == 1:
            dq_ref[:, cols] = turn_back(total, c, s).astype(jnp.bfloat16)
        else:
            total_ref[:, cols] = total

    def run(members, fresh):
        here = slice(0, len(members) * rows)
        for n, m in enumerate(members):
            k_ref[n * rows : (n + 1) * rows] = kv_refs[m][:, :HEAD_SIZE]
            v_ref[n * rows : (n + 1) * rows] = kv_refs[m][:, HEAD_SIZE:]
        k = k_ref[here]
        for h in range(group):
            lanes = slice(h * rows, (h + 1) * rows)
            p_ref[here, lanes], ds_ref[here, lanes] = fronts(
                rq_ref[:, cols_of(h)],
                do_ref[:, cols_of(h)],
                lse_ref[h : h + 1, :] * LOG2E,
                delta_ref[h : h + 1, :],
                k,
                v_ref[here],
            )
        gk = dot(ds_ref[here], stacked(rq_ref, group), NN) * LN2
        gv = dot(p_ref[here], stacked(do_ref, group), NN)
        for n, m in enumerate(members):
            own = slice(n * rows, (n + 1) * rows)
            dkv_refs[m][:, :HEAD_SIZE] = gk[own].astype(jnp.bfloat16)
            dkv_refs[m][:, HEAD_SIZE:] = gv[own].astype(jnp.bfloat16)
        for h in range(group):
            cols = cols_of(h)
            before = dq_in_ref[:, cols] if fresh else total_ref[:, cols]
            put(cols, before + dot(ds_ref[here, h * rows : (h + 1) * rows], k, TN))

    def skip(members, fresh):
        if fresh:
            for h in range(group):
                put(cols_of(h), dq_in_ref[:, cols_of(h)])
        for m in members:
            dkv_refs[m][...] = jnp.zeros_like(dkv_refs[m])

    start = 0
    for i, size in enumerate(joint):
        members = tuple(range(start, start + size))
        start += size
        pl.when(flag_ref[i] != 0)(functools.partial(run, members, i == 0))
        pl.when(flag_ref[i] == 0)(functools.partial(skip, members, i == 0))
    if final and sets > 1:
        for h in range(group):
            cols = cols_of(h)
            dq_ref[:, cols] = turn_back(total_ref[:, cols], c, s).astype(jnp.bfloat16)


def cross(kv_count, first, count, flags, joint, rq, do, lse, delta, c, s, dq, kvs, whole=None, final=False):
    rows, width = do.shape
    group = heads_of(width, kv_count)
    wide = group * HEAD_SIZE
    most = max(joint)
    big = pl.BlockSpec((rows, wide), lambda g, i: (0, g + first))
    row = pl.BlockSpec((group, rows), lambda g, i: (g + first, 0))
    table = pl.BlockSpec((rows, HEAD_SIZE), lambda g, i: (0, 0))
    pair = pl.BlockSpec((rows, 2 * HEAD_SIZE), lambda g, i: (0, g))
    shifted = pl.BlockSpec((rows, 2 * HEAD_SIZE), lambda g, i: (0, g + first))
    args = [flags, rq, do, lse, delta, c, s, dq, *kvs]
    in_specs = [big, big, row, row, table, table, big]
    chunk_width = count * 2 * HEAD_SIZE
    in_specs += [pair if x.shape[1] == chunk_width else shifted for x in kvs]
    mode = 0
    aliases = {}
    if final:
        mode = 1
        if whole is not None:
            mode = 2
            aliases = {len(args): 0}
            args.append(whole)
            in_specs.append(pl.BlockSpec(memory_space=pl.ANY))
    dq_shape = (
        jax.ShapeDtypeStruct((rows, width), jnp.bfloat16)
        if final
        else jax.ShapeDtypeStruct(dq.shape, jnp.float32)
    )
    return pl.pallas_call(
        functools.partial(cross_kernel, group, joint, mode),
        out_shape=[dq_shape]
        + [jax.ShapeDtypeStruct((rows, count * 2 * HEAD_SIZE), jnp.bfloat16)] * len(kvs),
        grid_spec=pltpu.PrefetchScalarGridSpec(
            num_scalar_prefetch=1,
            grid=(count,),
            in_specs=in_specs,
            out_specs=[big] + [pair] * len(kvs),
            scratch_shapes=[pltpu.VMEM((most * rows, group * rows), jnp.bfloat16)] * 2
            + [pltpu.VMEM((most * rows, HEAD_SIZE), jnp.bfloat16)] * 2
            + ([pltpu.VMEM((rows, wide), jnp.float32)] if final else []),
        ),
        input_output_aliases=aliases,
        compiler_params=params(1, 60),
        cost_estimate=pl.CostEstimate(
            flops=20 * count * group * rows * rows * HEAD_SIZE * len(kvs),
            bytes_accessed=rows * count * wide * 12,
            transcendentals=0,
        ),
        name="cross",
    )(*args)


def settle_kernel(own_ref, c_ref, s_ref, *refs):
    *in_refs, o_ref = refs
    c, s = c_ref[...], s_ref[...]
    for b in range(0, o_ref.shape[1], 2 * HEAD_SIZE):
        k, v = slice(b, b + HEAD_SIZE), slice(b + HEAD_SIZE, b + 2 * HEAD_SIZE)
        gk, gv = own_ref[:, k], own_ref[:, v]
        for ref in in_refs:
            gk = gk + ref[:, k].astype(jnp.float32)
            gv = gv + ref[:, v].astype(jnp.float32)
        o_ref[:, k] = turn_back(gk, c, s)
        o_ref[:, v] = gv


def settle(local, parts, c, s):
    return pl.pallas_call(
        settle_kernel,
        out_shape=jax.ShapeDtypeStruct(local.shape, jnp.float32),
        compiler_params=params(0, 60),
        name="settle",
    )(local, c, s, *parts)


def finish_kernel(own_ref, children_ref, dk_ref, dv_ref):
    for g in range(dk_ref.shape[1] // HEAD_SIZE):
        a, b = g * HEAD_SIZE, 2 * g * HEAD_SIZE
        total = own_ref[:, b : b + 2 * HEAD_SIZE]
        total = total + children_ref[:, b : b + 2 * HEAD_SIZE].astype(jnp.float32)
        dk_ref[:, a : a + HEAD_SIZE] = total[:, :HEAD_SIZE].astype(jnp.bfloat16)
        dv_ref[:, a : a + HEAD_SIZE] = total[:, HEAD_SIZE:].astype(jnp.bfloat16)


def finish(base, children):
    rows, width = base.shape
    return pl.pallas_call(
        finish_kernel,
        out_shape=[jax.ShapeDtypeStruct((rows, width // 2), jnp.bfloat16)] * 2,
        compiler_params=params(0, 8),
        name="finish",
    )(base, children)


def body(
    queries,
    unrotated_keys,
    value_rows,
    outputs,
    output_gradient,
    saved_logsumexp,
    ancestors,
    placement,
    positions,
):
    hops = lax.axis_size("head")
    places = lax.axis_size("ctx")
    here = lax.axis_index("ctx")
    me = lax.axis_index("head")
    rows = queries.shape[0]
    assert rows * hops == TREE_BLOCK and placement.shape[0] == places
    c, s = rope_tables(positions)

    match = ancestors[placement][:, :1] == placement[None, :]
    source = jnp.argmax(match, axis=1).astype(jnp.int32)
    present = jnp.any(match, axis=1).astype(jnp.int32)

    kv_count = unrotated_keys.shape[1] // HEAD_SIZE
    sizes = split(kv_count)
    chunks = range(len(sizes))
    firsts = [sum(sizes[:g]) for g in chunks]

    def exchange(x):
        width = x.shape[-1]
        return lax.all_to_all(
            x.reshape(places, rows // places, width), "ctx", 0, 0, tiled=True
        )

    def shift(x, n, wrap):
        route = [(i, (i + n) % hops) for i in range(hops) if wrap or 0 <= i + n < hops]
        return lax.ppermute(x, "head", route)

    raw = pair(unrotated_keys, value_rows)
    own_flags = jnp.stack([(me >= n).astype(jnp.int32) for n in range(1, hops)])
    parent_flag = present[here][None]

    piece_rows = rows // places
    offset = me * rows + here * piece_rows + jnp.arange(piece_rows, dtype=jnp.int32)
    middle_at = (TREE_BLOCK * placement[:, None] + offset[None, :]).reshape(-1)
    middle_c, middle_s = [
        t.reshape(places, piece_rows, HEAD_SIZE) for t in rope_tables(middle_at)
    ]

    middle = exchange(raw)
    kv = turn_keys(raw, c, s)
    own_kv = [shift(kv, n, False) for n in range(1, hops)]
    rq, delta, dq, local = diagonal(
        queries, output_gradient, outputs, saved_logsumexp, c, s, kv
    )
    picked = pick(source, middle, middle_c, middle_s)
    near = exchange(picked).reshape(rows, -1)
    dq, *own_part = cross(
        kv_count, 0, kv_count, own_flags, (1,) * (hops - 1), rq, output_gradient,
        saved_logsumexp, delta, c, s, dq, own_kv,
    )
    back = [shift(own_part[n - 1], -n, False) for n in range(1, hops)]
    base = settle(local, back, c, s)

    far = []
    for g in chunks:
        at = 2 * HEAD_SIZE * firsts[g]
        piece = near[:, at : at + 2 * HEAD_SIZE * sizes[g]]
        far.append([shift(piece, n, True) for n in range(1, hops)])

    def tiles(g, dq, kvs, whole, final):
        return cross(
            kv_count, firsts[g], sizes[g], parent_flag, (len(kvs),), rq, output_gradient,
            saved_logsumexp, delta, c, s, dq, kvs, whole, final,
        )

    grad_queries = None
    ups = []
    for g in chunks:
        part = dq
        if g == 0:
            part, near_part = tiles(g, part, [near], None, False)
        part, *far_part = tiles(g, part, far[g], grad_queries, g == 0)
        if g:
            part, near_part = tiles(g, part, [near], grad_queries, True)
        grad_queries = part
        joined = [shift(x, -n - 1, True) for n, x in enumerate(far_part)]
        total = near_part.astype(jnp.float32)
        for x in joined:
            total = total + x.astype(jnp.float32)
        send = total.astype(jnp.bfloat16)
        if g:
            send, ups[-1] = lax.optimization_barrier((send, ups[-1]))
        ups.append(exchange(send))
    merged = merge(source, present, middle_c, middle_s, ups)
    children = exchange(merged).reshape(rows, -1)
    grad_keys, grad_values = finish(base, children)
    return (grad_queries, grad_keys, grad_values)


def split(kv_count):
    return (kv_count // 2, kv_count - kv_count // 2)


def solution(mesh):
    return jax.shard_map(
        body,
        mesh=mesh,
        in_specs=(
            P(("ctx", "head"), None),
            P(("ctx", "head"), None),
            P(("ctx", "head"), None),
            P(("ctx", "head"), None),
            P(("ctx", "head"), None),
            P(None, ("ctx", "head")),
            P(),
            P(),
            P(("ctx", "head")),
        ),
        out_specs=(P(("ctx", "head"), None), P(("ctx", "head"), None), P(("ctx", "head"), None)),
        check_vma=False,
    )
```

```python
import functools
import math

import jax
import jax.numpy as jnp
from jax import lax
from jax.experimental import pallas as pl
from jax.experimental.pallas import tpu as pltpu
from jax.sharding import PartitionSpec as P


HEAD_SIZE = 128
TREE_BLOCK = 512
LOG2E = math.log2(math.e)
LN2 = math.log(2.0)
SCALE = 1.0 / math.sqrt(HEAD_SIZE)
rope_base = 500000.0
MIB = 1024 * 1024
NT = (((1,), (1,)), ((), ()))
NN = (((1,), (0,)), ((), ()))
TN = (((0,), (0,)), ((), ()))


def rope_tables(positions):
    half_dim = HEAD_SIZE // 2
    freq_index = jnp.arange(half_dim, dtype=jnp.float32)
    inverse = rope_base ** (-(2.0 * freq_index / HEAD_SIZE))
    angles = positions.astype(jnp.float32)[:, None] * inverse[None, :]
    c, s = jnp.cos(angles), jnp.sin(angles)
    return jnp.concatenate([c, c], -1), jnp.concatenate([-s, s], -1)


def dot(a, b, dims):
    return lax.dot_general(a, b, dims, preferred_element_type=jnp.float32)


def turn(x, c, s):
    return x * c + pltpu.roll(x, HEAD_SIZE // 2, 1) * s


def turn_back(x, c, s):
    return x * c - pltpu.roll(x, HEAD_SIZE // 2, 1) * s


def params(n, mib):
    return pltpu.CompilerParams(
        dimension_semantics=("arbitrary",) * n, vmem_limit_bytes=mib * MIB
    )


def find_slots(place_ref, slot_ref):
    for b in range(place_ref.shape[0]):
        slot_ref[place_ref[b]] = b


def pick_kernel(place_ref, anc_ref, x_ref, c_ref, s_ref, *refs):
    *o_refs, slot_ref = refs
    find_slots(place_ref, slot_ref)
    half = x_ref.shape[2] // 2
    for d in range(x_ref.shape[0]):
        at = slot_ref[jnp.maximum(anc_ref[place_ref[d]], 0)]
        c, s = c_ref[at], s_ref[at]
        a = 0
        for o_ref in o_refs:
            for b in range(0, o_ref.shape[2], 2 * HEAD_SIZE):
                x = x_ref[at, :, a : a + HEAD_SIZE].astype(jnp.float32)
                o_ref[d, :, b : b + HEAD_SIZE] = turn(x, c, s).astype(jnp.bfloat16)
                o_ref[d, :, b + HEAD_SIZE : b + 2 * HEAD_SIZE] = x_ref[
                    at, :, half + a : half + a + HEAD_SIZE
                ]
                a += HEAD_SIZE


def pick(sizes, places, ancestors, x, c, s):
    return pl.pallas_call(
        pick_kernel,
        out_shape=[
            jax.ShapeDtypeStruct(x.shape[:2] + (size * 2 * HEAD_SIZE,), x.dtype) for size in sizes
        ],
        in_specs=[pl.BlockSpec(memory_space=pltpu.SMEM)] * 2
        + [pl.BlockSpec(memory_space=pltpu.VMEM)] * 3,
        out_specs=[pl.BlockSpec(memory_space=pltpu.VMEM)] * len(sizes),
        scratch_shapes=[pltpu.SMEM(places.shape, jnp.int32)],
        compiler_params=params(0, 8),
        name="pick",
    )(places, ancestors, x, c, s)


def merge_kernel(place_ref, anc_ref, c_ref, s_ref, *refs):
    *x_refs, o_ref, acc_ref, slot_ref = refs
    find_slots(place_ref, slot_ref)
    acc_ref[...] = jnp.zeros_like(acc_ref)
    for d in range(o_ref.shape[0]):

        above = anc_ref[place_ref[d]]

        @pl.when(above >= 0)
        def _():
            into, at = slot_ref[jnp.maximum(above, 0)], 0
            for x_ref in x_refs:
                width = x_ref.shape[2]
                acc_ref[into, :, at : at + width] += x_ref[d].astype(jnp.float32)
                at += width

    for d in range(o_ref.shape[0]):
        c, s = c_ref[d], s_ref[d]
        for b in range(0, o_ref.shape[2], 2 * HEAD_SIZE):
            k, v = slice(b, b + HEAD_SIZE), slice(b + HEAD_SIZE, b + 2 * HEAD_SIZE)
            o_ref[d, :, k] = turn_back(acc_ref[d, :, k], c, s).astype(o_ref.dtype)
            o_ref[d, :, v] = acc_ref[d, :, v].astype(o_ref.dtype)


def merge(places, ancestors, c, s, xs):
    shape = xs[0].shape[:2] + (sum(x.shape[2] for x in xs),)
    return pl.pallas_call(
        merge_kernel,
        out_shape=jax.ShapeDtypeStruct(shape, xs[0].dtype),
        in_specs=[pl.BlockSpec(memory_space=pltpu.SMEM)] * 2
        + [pl.BlockSpec(memory_space=pltpu.VMEM)] * (2 + len(xs)),
        out_specs=pl.BlockSpec(memory_space=pltpu.VMEM),
        scratch_shapes=[pltpu.VMEM(shape, jnp.float32), pltpu.SMEM(places.shape, jnp.int32)],
        compiler_params=params(0, 10),
        name="merge",
    )(places, ancestors, c, s, *xs)


def fronts(rq, do, lse, delta, k, v, mask=None):
    prob = jnp.exp2(dot(k, rq, NT) - lse)
    if mask is not None:
        prob = jnp.where(mask, prob, 0.0)
    grad_score = prob * (dot(v, do, NT) - delta)
    return prob.astype(jnp.bfloat16), grad_score.astype(jnp.bfloat16)


def stacked(ref, group):
    return jnp.concatenate([ref[:, cols_of(h)] for h in range(group)], 0)


def heads_of(width, kv_count):
    return width // HEAD_SIZE // kv_count


def cols_of(h):
    return slice(h * HEAD_SIZE, (h + 1) * HEAD_SIZE)


def diagonal_kernel(group, q_ref, do_ref, out_ref, lse_ref, c_ref, s_ref, raw_ref, v_ref, rq_ref, delta_ref, dq_ref, dkv_ref, p_ref, ds_ref):
    rows = q_ref.shape[0]
    c, s = c_ref[...] * (SCALE * LOG2E), s_ref[...] * (SCALE * LOG2E)
    key_at = lax.broadcasted_iota(jnp.int32, (rows, rows), 0)
    query_at = lax.broadcasted_iota(jnp.int32, (rows, rows), 1)
    causal = key_at <= query_at
    k = turn(raw_ref[...].astype(jnp.float32), c_ref[...], s_ref[...]).astype(jnp.bfloat16)
    v = v_ref[...]
    for h in range(group):
        cols, lanes = cols_of(h), slice(h * rows, (h + 1) * rows)
        do = do_ref[:, cols]
        rq = turn(q_ref[:, cols].astype(jnp.float32), c, s).astype(jnp.bfloat16)
        rq_ref[:, cols] = rq
        product = do.astype(jnp.float32) * out_ref[:, cols].astype(jnp.float32)
        delta = jnp.sum(product.T, axis=0, keepdims=True)
        delta_ref[h : h + 1, :] = delta
        p_ref[:, lanes], ds_ref[:, lanes] = fronts(
            rq, do, lse_ref[h : h + 1, :] * LOG2E, delta, k, v, causal
        )
    dkv_ref[:, :HEAD_SIZE] = dot(ds_ref[...], stacked(rq_ref, group), NN) * LN2
    dkv_ref[:, HEAD_SIZE:] = dot(p_ref[...], stacked(do_ref, group), NN)
    for h in range(group):
        gq = dot(ds_ref[:, h * rows : (h + 1) * rows], k, TN)
        dq_ref[:, cols_of(h)] = gq.astype(jnp.bfloat16)


def diagonal(q, do, out, lse, c, s, keys, values):
    rows, width = q.shape
    kv_count = count = keys.shape[1] // HEAD_SIZE
    first = 0
    group = heads_of(width, kv_count)
    wide = group * HEAD_SIZE
    big = pl.BlockSpec((rows, wide), lambda g: (0, g + first))
    row = pl.BlockSpec((group, rows), lambda g: (g + first, 0))
    table = pl.BlockSpec((rows, HEAD_SIZE), lambda g: (0, 0))
    pair = pl.BlockSpec((rows, 2 * HEAD_SIZE), lambda g: (0, g))
    one = pl.BlockSpec((rows, HEAD_SIZE), lambda g: (0, g))
    part = pl.BlockSpec((rows, wide), lambda g: (0, g))
    part_row = pl.BlockSpec((group, rows), lambda g: (g, 0))
    return pl.pallas_call(
        functools.partial(diagonal_kernel, group),
        out_shape=[
            jax.ShapeDtypeStruct((rows, count * wide), jnp.bfloat16),
            jax.ShapeDtypeStruct((count * group, rows), jnp.float32),
            jax.ShapeDtypeStruct((rows, count * wide), jnp.bfloat16),
            jax.ShapeDtypeStruct((rows, count * 2 * HEAD_SIZE), jnp.float32),
        ],
        grid=(count,),
        in_specs=[big, big, big, row, table, table, one, one],
        out_specs=[part, part_row, part, pair],
        scratch_shapes=[pltpu.VMEM((rows, group * rows), jnp.bfloat16)] * 2,
        compiler_params=params(1, 60),
        cost_estimate=pl.CostEstimate(
            flops=20 * count * group * rows * rows * HEAD_SIZE,
            bytes_accessed=rows * count * wide * 12,
            transcendentals=0,
        ),
        name="diagonal",
    )(q, do, out, lse, c, s, keys, values)


def cross_kernel(group, joint, final, ours, info_ref, place_ref, anc_ref, rq_ref, do_ref, lse_ref, delta_ref, c_ref, s_ref, dq_in_ref, *refs):
    sets = len(joint)
    refs = list(refs)
    kv_refs = [[refs.pop(0) for _ in range(4 if ours else 1)] for _ in range(sum(joint))]
    if final == 2:
        refs.pop(0)
    dq_ref = refs.pop(0)
    dkv_refs = [refs.pop(0) for _ in range(sum(joint))]
    p_ref, ds_ref, k_ref, v_ref = refs[:4]
    total_ref = refs[4] if sets > 1 else None
    rows = rq_ref.shape[0]
    c, s = c_ref[...] * SCALE, s_ref[...] * SCALE

    def put(cols, total):
        if final and sets == 1:
            dq_ref[:, cols] = turn_back(total, c, s).astype(jnp.bfloat16)
        elif sets == 1:
            dq_ref[:, cols] = total.astype(jnp.bfloat16)
        else:
            total_ref[:, cols] = total

    def run(members, fresh):
        here = slice(0, len(members) * rows)
        for n, m in enumerate(members):
            at = slice(n * rows, (n + 1) * rows)
            if ours:
                raw_ref, values_ref, kc_ref, ks_ref = kv_refs[m]
                raw = raw_ref[...].astype(jnp.float32)
                k_ref[at] = turn(raw, kc_ref[...], ks_ref[...]).astype(jnp.bfloat16)
                v_ref[at] = values_ref[...]
            else:
                k_ref[at] = kv_refs[m][0][:, :HEAD_SIZE]
                v_ref[at] = kv_refs[m][0][:, HEAD_SIZE:]
        k = k_ref[here]
        for h in range(group):
            lanes = slice(h * rows, (h + 1) * rows)
            p_ref[here, lanes], ds_ref[here, lanes] = fronts(
                rq_ref[:, cols_of(h)],
                do_ref[:, cols_of(h)],
                lse_ref[h : h + 1, :] * LOG2E,
                delta_ref[h : h + 1, :],
                k,
                v_ref[here],
            )
        gk = dot(ds_ref[here], stacked(rq_ref, group), NN) * LN2
        gv = dot(p_ref[here], stacked(do_ref, group), NN)
        for n, m in enumerate(members):
            own = slice(n * rows, (n + 1) * rows)
            dkv_refs[m][:, :HEAD_SIZE] = gk[own].astype(jnp.bfloat16)
            dkv_refs[m][:, HEAD_SIZE:] = gv[own].astype(jnp.bfloat16)
        for h in range(group):
            cols = cols_of(h)
            before = dq_in_ref[:, cols].astype(jnp.float32) if fresh else total_ref[:, cols]
            put(cols, before + dot(ds_ref[here, h * rows : (h + 1) * rows], k, TN))

    def skip(members, fresh):
        if fresh:
            for h in range(group):
                put(cols_of(h), dq_in_ref[:, cols_of(h)].astype(jnp.float32))
        for m in members:
            dkv_refs[m][...] = jnp.zeros_like(dkv_refs[m])

    start = 0
    for i, size in enumerate(joint):
        members = tuple(range(start, start + size))
        start += size
        if ours:
            counts = info_ref[0] > i
        else:
            counts = anc_ref[place_ref[info_ref[1]]] >= 0
        pl.when(counts)(functools.partial(run, members, i == 0))
        pl.when(jnp.logical_not(counts))(functools.partial(skip, members, i == 0))
    if sets > 1:
        for h in range(group):
            total = total_ref[:, cols_of(h)]
            if final:
                total = turn_back(total, c, s)
            dq_ref[:, cols_of(h)] = total.astype(jnp.bfloat16)


def cross(kv_count, first, count, tree, ours, joint, rq, do, lse, delta, c, s, dq, kvs, whole=None, final=False):
    rows, width = do.shape
    group = heads_of(width, kv_count)
    wide = group * HEAD_SIZE
    most = max(joint)
    big = pl.BlockSpec((rows, wide), lambda g, *_: (0, g + first))
    row = pl.BlockSpec((group, rows), lambda g, *_: (g + first, 0))
    table = pl.BlockSpec((rows, HEAD_SIZE), lambda g, *_: (0, 0))
    pair = pl.BlockSpec((rows, 2 * HEAD_SIZE), lambda g, *_: (0, g))
    args = [*tree, rq, do, lse, delta, c, s, dq]
    args += [x for x in kvs] if not ours else [y for x, kc, ks in kvs for y in (x, x, kc, ks)]
    in_specs = [big, big, row, row, table, table, big]
    if ours:
        keys_at = pl.BlockSpec((rows, HEAD_SIZE), lambda g, *_: (0, g + first))
        values_at = pl.BlockSpec((rows, HEAD_SIZE), lambda g, *_: (0, g + first + kv_count))
        in_specs += [keys_at, values_at, table, table] * len(kvs)
    else:
        in_specs += [pair] * len(kvs)
    mode = 0
    aliases = {}
    if final:
        mode = 1
        if whole is not None:
            mode = 2
            aliases = {len(args): 0}
            args.append(whole)
            in_specs.append(pl.BlockSpec(memory_space=pl.ANY))
    dq_shape = (
        jax.ShapeDtypeStruct((rows, width), jnp.bfloat16)
        if final
        else jax.ShapeDtypeStruct(dq.shape, jnp.bfloat16)
    )
    return pl.pallas_call(
        functools.partial(cross_kernel, group, joint, mode, ours),
        out_shape=[dq_shape]
        + [jax.ShapeDtypeStruct((rows, count * 2 * HEAD_SIZE), jnp.bfloat16)] * len(kvs),
        grid_spec=pltpu.PrefetchScalarGridSpec(
            num_scalar_prefetch=3,
            grid=(count,),
            in_specs=in_specs,
            out_specs=[big] + [pair] * len(kvs),
            scratch_shapes=[pltpu.VMEM((most * rows, group * rows), jnp.bfloat16)] * 2
            + [pltpu.VMEM((most * rows, HEAD_SIZE), jnp.bfloat16)] * 2
            + ([pltpu.VMEM((rows, wide), jnp.float32)] if len(joint) > 1 else []),
        ),
        input_output_aliases=aliases,
        compiler_params=params(1, 60),
        cost_estimate=pl.CostEstimate(
            flops=20 * count * group * rows * rows * HEAD_SIZE * len(kvs),
            bytes_accessed=rows * count * wide * 12,
            transcendentals=0,
        ),
        name="cross",
    )(*args)


def settle_kernel(counts, own_ref, c_ref, s_ref, *refs):
    *in_refs, o_ref = refs
    c, s = c_ref[...], s_ref[...]
    a = 0
    for count in counts:
        mine, in_refs = in_refs[:count], in_refs[count:]
        for b in range(0, mine[0].shape[1], 2 * HEAD_SIZE):
            total = own_ref[:, a : a + 2 * HEAD_SIZE]
            for ref in mine:
                total = total + ref[:, b : b + 2 * HEAD_SIZE].astype(jnp.float32)
            o_ref[:, a : a + HEAD_SIZE] = turn_back(total[:, :HEAD_SIZE], c, s)
            o_ref[:, a + HEAD_SIZE : a + 2 * HEAD_SIZE] = total[:, HEAD_SIZE:]
            a += 2 * HEAD_SIZE


def settle(local, chunks, c, s):
    return pl.pallas_call(
        functools.partial(settle_kernel, [len(x) for x in chunks]),
        out_shape=jax.ShapeDtypeStruct(local.shape, jnp.float32),
        compiler_params=params(0, 12),
        name="settle",
    )(local, c, s, *[x for chunk in chunks for x in chunk])


def finish_kernel(own_ref, children_ref, dk_ref, dv_ref):
    for g in range(dk_ref.shape[1] // HEAD_SIZE):
        a, b = g * HEAD_SIZE, 2 * g * HEAD_SIZE
        total = own_ref[:, b : b + 2 * HEAD_SIZE]
        total = total + children_ref[:, b : b + 2 * HEAD_SIZE].astype(jnp.float32)
        dk_ref[:, a : a + HEAD_SIZE] = total[:, :HEAD_SIZE].astype(jnp.bfloat16)
        dv_ref[:, a : a + HEAD_SIZE] = total[:, HEAD_SIZE:].astype(jnp.bfloat16)


def finish(base, children):
    rows, width = base.shape
    return pl.pallas_call(
        finish_kernel,
        out_shape=[jax.ShapeDtypeStruct((rows, width // 2), jnp.bfloat16)] * 2,
        compiler_params=params(0, 8),
        name="finish",
    )(base, children)


def body(
    queries,
    unrotated_keys,
    value_rows,
    outputs,
    output_gradient,
    saved_logsumexp,
    ancestors,
    placement,
    positions,
):
    hops = lax.axis_size("head")
    places = lax.axis_size("ctx")
    here = lax.axis_index("ctx")
    me = lax.axis_index("head")
    rows = queries.shape[0]
    assert rows * hops == TREE_BLOCK and placement.shape[0] == places
    assert ancestors.shape[1] == 1
    c, s = rope_tables(positions)

    parents = ancestors.reshape(-1)
    tree = (jnp.stack([me, here]).astype(jnp.int32), placement, parents)

    kv_count = unrotated_keys.shape[1] // HEAD_SIZE
    sizes = split(kv_count)
    chunks = range(len(sizes))
    firsts = [sum(sizes[:g]) for g in chunks]

    def exchange(x):
        width = x.shape[-1]
        return lax.all_to_all(
            x.reshape(places, rows // places, width), "ctx", 0, 0, tiled=True
        )

    def shift(x, n, wrap):
        route = [(i, (i + n) % hops) for i in range(hops) if wrap or 0 <= i + n < hops]
        return lax.ppermute(x, "head", route)

    raw = jnp.concatenate([unrotated_keys, value_rows], 1)

    piece_rows = rows // places
    offset = me * rows + here * piece_rows + jnp.arange(piece_rows, dtype=jnp.int32)
    middle_at = (TREE_BLOCK * placement[:, None] + offset[None, :]).reshape(-1)
    middle_c, middle_s = [
        t.reshape(places, piece_rows, HEAD_SIZE) for t in rope_tables(middle_at)
    ]

    middle = exchange(raw)
    own_kv = [(shift(raw, n, False), *rope_tables(positions - n * rows)) for n in range(1, hops)]
    rq, delta, dq, local = diagonal(
        queries, output_gradient, outputs, saved_logsumexp, c, s, unrotated_keys, value_rows
    )
    picked = pick(sizes, placement, parents, middle, middle_c, middle_s)
    near = []
    for g in chunks:
        send = picked[g]
        if g:
            send, near[-1] = lax.optimization_barrier((send, near[-1]))
        near.append(exchange(send))
    near = [x.reshape(rows, -1) for x in near]

    far = []
    for g in chunks:
        far.append([shift(near[g], n, True) for n in range(1, hops)])

    def tiles(g, dq, kvs, ours, joint, whole=None, final=False):
        return cross(
            kv_count, firsts[g], sizes[g], tree, ours, joint, rq, output_gradient,
            saved_logsumexp, delta, c, s, dq, kvs, whole, final,
        )

    grad_queries = None
    ups, backs = [], []
    for g in chunks:

        def peers(part, *rest):
            return tiles(g, part, own_kv, True, (1,) * (hops - 1), *rest)

        def parent(part, *rest):
            return tiles(g, part, [near[g]], False, (1,), *rest)

        def beyond(part, *rest):
            return tiles(g, part, far[g], False, (hops - 1,), *rest)

        if g == 0:
            part, *own_part = peers(dq)
            part, near_part = parent(part)
            grad_queries, *far_part = beyond(part, None, True)
        else:
            part, *far_part = beyond(dq)
            part, near_part = parent(part)
            grad_queries, *own_part = peers(part, grad_queries, True)
        backs.append([shift(x, -n - 1, False) for n, x in enumerate(own_part)])
        joined = [shift(x, -n - 1, True) for n, x in enumerate(far_part)]
        total = near_part.astype(jnp.float32)
        for x in joined:
            total = total + x.astype(jnp.float32)
        send = total.astype(jnp.bfloat16)
        if g:
            send, ups[-1] = lax.optimization_barrier((send, ups[-1]))
        ups.append(exchange(send))
    base = settle(local, backs, c, s)
    merged = merge(placement, parents, middle_c, middle_s, ups)
    children = exchange(merged).reshape(rows, -1)
    grad_keys, grad_values = finish(base, children)
    return (grad_queries, grad_keys, grad_values)


def split(kv_count):
    return (kv_count // 2, kv_count - kv_count // 2)


def solution(mesh):
    return jax.shard_map(
        body,
        mesh=mesh,
        in_specs=(
            P(("ctx", "head"), None),
            P(("ctx", "head"), None),
            P(("ctx", "head"), None),
            P(("ctx", "head"), None),
            P(("ctx", "head"), None),
            P(None, ("ctx", "head")),
            P(),
            P(),
            P(("ctx", "head")),
        ),
        out_specs=(P(("ctx", "head"), None), P(("ctx", "head"), None), P(("ctx", "head"), None)),
        check_vma=False,
    )
```

```python
import functools
import math

import jax
import jax.numpy as jnp
from jax import lax
from jax.experimental import pallas as pl
from jax.experimental.pallas import tpu as pltpu
from jax.sharding import PartitionSpec as P


HEAD_SIZE = 128
TREE_BLOCK = 512
LOG2E = math.log2(math.e)
LN2 = math.log(2.0)
SCALE = 1.0 / math.sqrt(HEAD_SIZE)
rope_base = 500000.0
MIB = 1024 * 1024
NT = (((1,), (1,)), ((), ()))
NN = (((1,), (0,)), ((), ()))
TN = (((0,), (0,)), ((), ()))


def rope_tables(positions):
    lane = jnp.arange(HEAD_SIZE, dtype=jnp.int32)
    half_dim = HEAD_SIZE // 2
    freq_index = (lane % half_dim).astype(jnp.float32)
    inverse = rope_base ** (-(2.0 * freq_index / HEAD_SIZE))
    angles = positions.astype(jnp.float32)[:, None] * inverse[None, :]
    sign = jnp.where(lane < half_dim, -1.0, 1.0)
    return jnp.cos(angles), jnp.sin(angles) * sign[None, :]


def dot(a, b, dims):
    return lax.dot_general(a, b, dims, preferred_element_type=jnp.float32)


def turn(x, c, s):
    return x * c + pltpu.roll(x, HEAD_SIZE // 2, 1) * s


def turn_back(x, c, s):
    return x * c - pltpu.roll(x, HEAD_SIZE // 2, 1) * s


def params(n, mib):
    return pltpu.CompilerParams(
        dimension_semantics=("arbitrary",) * n, vmem_limit_bytes=mib * MIB
    )


def side_kernel(pieces, k_ref, v_ref, o_ref, buf, sem_in, sem_out):
    rows, width = k_ref.shape
    step = rows // pieces
    ins, outs = [], []
    for i in range(2 * pieces):
        part, x_ref = i // pieces, (k_ref, v_ref)[i // pieces]
        at = pl.ds((i % pieces) * step, step)
        to = o_ref.at[at, pl.ds(part * width, width)]
        ins.append(pltpu.make_async_copy(x_ref.at[at], buf.at[i], sem_in.at[i]))
        outs.append(pltpu.make_async_copy(buf.at[i], to, sem_out.at[i]))
    for copy in ins:
        copy.start()
    for before, after in zip(ins, outs):
        before.wait()
        after.start()
    for copy in outs:
        copy.wait()


def side(keys, values):
    rows, width = keys.shape
    pieces = 2
    return pl.pallas_call(
        functools.partial(side_kernel, pieces),
        out_shape=jax.ShapeDtypeStruct((rows, 2 * width), keys.dtype),
        in_specs=[pl.BlockSpec(memory_space=pl.ANY)] * 2,
        out_specs=pl.BlockSpec(memory_space=pl.ANY),
        scratch_shapes=[
            pltpu.VMEM((2 * pieces, rows // pieces, width), keys.dtype),
            pltpu.SemaphoreType.DMA((2 * pieces,)),
            pltpu.SemaphoreType.DMA((2 * pieces,)),
        ],
        compiler_params=params(0, 60),
        name="side",
    )(keys, values)


def find_slots(place_ref, slot_ref):
    for b in range(place_ref.shape[0]):
        slot_ref[place_ref[b]] = b


def pick_kernel(copies, place_ref, anc_ref, x_ref, c_ref, s_ref, *refs):
    *o_refs, slot_ref = refs
    find_slots(place_ref, slot_ref)
    half = x_ref.shape[2] // 2
    for d in range(x_ref.shape[0]):
        at = slot_ref[jnp.maximum(anc_ref[place_ref[d]], 0)]
        c, s = c_ref[at], s_ref[at]
        a = 0
        for o_ref, times in zip(o_refs, copies):
            for b in range(0, o_ref.shape[2], 2 * HEAD_SIZE):
                x = x_ref[at, :, a : a + HEAD_SIZE].astype(jnp.float32)
                k = turn(x, c, s).astype(jnp.bfloat16)
                v = x_ref[at, :, half + a : half + a + HEAD_SIZE]
                for n in range(d * times, (d + 1) * times):
                    o_ref[n, :, b : b + HEAD_SIZE] = k
                    o_ref[n, :, b + HEAD_SIZE : b + 2 * HEAD_SIZE] = v
                a += HEAD_SIZE


def pick(sizes, copies, places, ancestors, x, c, s):
    return pl.pallas_call(
        functools.partial(pick_kernel, copies),
        out_shape=[
            jax.ShapeDtypeStruct((x.shape[0] * n, x.shape[1], size * 2 * HEAD_SIZE), x.dtype)
            for size, n in zip(sizes, copies)
        ],
        in_specs=[pl.BlockSpec(memory_space=pltpu.SMEM)] * 2
        + [pl.BlockSpec(memory_space=pltpu.VMEM)] * 3,
        out_specs=[pl.BlockSpec(memory_space=pltpu.VMEM)] * len(sizes),
        scratch_shapes=[pltpu.SMEM(places.shape, jnp.int32)],
        compiler_params=params(0, 8),
        name="pick",
    )(places, ancestors, x, c, s)


def merge_kernel(place_ref, anc_ref, c_ref, s_ref, *refs):
    *x_refs, o_ref, acc_ref, slot_ref = refs
    find_slots(place_ref, slot_ref)
    acc_ref[...] = jnp.zeros_like(acc_ref)
    for d in range(o_ref.shape[0]):

        above = anc_ref[place_ref[d]]

        @pl.when(above >= 0)
        def _():
            into, at = slot_ref[jnp.maximum(above, 0)], 0
            for x_ref in x_refs:
                width = x_ref.shape[2]
                acc_ref[into, :, at : at + width] += x_ref[d].astype(jnp.float32)
                at += width

    for d in range(o_ref.shape[0]):
        c, s = c_ref[d], s_ref[d]
        for b in range(0, o_ref.shape[2], 2 * HEAD_SIZE):
            k, v = slice(b, b + HEAD_SIZE), slice(b + HEAD_SIZE, b + 2 * HEAD_SIZE)
            o_ref[d, :, k] = turn_back(acc_ref[d, :, k], c, s).astype(o_ref.dtype)
            o_ref[d, :, v] = acc_ref[d, :, v].astype(o_ref.dtype)


def merge(places, ancestors, c, s, xs):
    shape = xs[0].shape[:2] + (sum(x.shape[2] for x in xs),)
    return pl.pallas_call(
        merge_kernel,
        out_shape=jax.ShapeDtypeStruct(shape, xs[0].dtype),
        in_specs=[pl.BlockSpec(memory_space=pltpu.SMEM)] * 2
        + [pl.BlockSpec(memory_space=pltpu.VMEM)] * (2 + len(xs)),
        out_specs=pl.BlockSpec(memory_space=pltpu.VMEM),
        scratch_shapes=[pltpu.VMEM(shape, jnp.float32), pltpu.SMEM(places.shape, jnp.int32)],
        compiler_params=params(0, 10),
        name="merge",
    )(places, ancestors, c, s, *xs)


def fronts(rq, do, lse, delta, k, v, mask=None):
    prob = jnp.exp2(dot(k, rq, NT) - lse)
    if mask is not None:
        prob = jnp.where(mask, prob, 0.0)
    grad_score = prob * (dot(v, do, NT) - delta)
    return prob.astype(jnp.bfloat16), grad_score.astype(jnp.bfloat16)


def stacked(ref, group):
    return jnp.concatenate([ref[:, cols_of(h)] for h in range(group)], 0)


def heads_of(width, kv_count):
    return width // HEAD_SIZE // kv_count


def cols_of(h):
    return slice(h * HEAD_SIZE, (h + 1) * HEAD_SIZE)


def diagonal_kernel(group, q_ref, do_ref, out_ref, lse_ref, c_ref, s_ref, raw_ref, v_ref, rq_ref, delta_ref, dq_ref, dkv_ref, p_ref, ds_ref):
    rows = q_ref.shape[0]
    c, s = c_ref[...] * (SCALE * LOG2E), s_ref[...] * (SCALE * LOG2E)
    key_at = lax.broadcasted_iota(jnp.int32, (rows, rows), 0)
    query_at = lax.broadcasted_iota(jnp.int32, (rows, rows), 1)
    causal = key_at <= query_at
    k = turn(raw_ref[...].astype(jnp.float32), c_ref[...], s_ref[...]).astype(jnp.bfloat16)
    v = v_ref[...]
    for h in range(group):
        cols, lanes = cols_of(h), slice(h * rows, (h + 1) * rows)
        do = do_ref[:, cols]
        rq = turn(q_ref[:, cols].astype(jnp.float32), c, s).astype(jnp.bfloat16)
        rq_ref[:, cols] = rq
        product = do.astype(jnp.float32) * out_ref[:, cols].astype(jnp.float32)
        delta = jnp.sum(product.T, axis=0, keepdims=True)
        delta_ref[h : h + 1, :] = delta
        p_ref[:, lanes], ds_ref[:, lanes] = fronts(
            rq, do, lse_ref[h : h + 1, :] * LOG2E, delta, k, v, causal
        )
    dkv_ref[:, :HEAD_SIZE] = dot(ds_ref[...], stacked(rq_ref, group), NN) * LN2
    dkv_ref[:, HEAD_SIZE:] = dot(p_ref[...], stacked(do_ref, group), NN)
    for h in range(group):
        gq = dot(ds_ref[:, h * rows : (h + 1) * rows], k, TN)
        dq_ref[:, cols_of(h)] = gq.astype(jnp.bfloat16)


def diagonal(q, do, out, lse, c, s, keys, values):
    rows, width = q.shape
    kv_count = count = keys.shape[1] // HEAD_SIZE
    first = 0
    group = heads_of(width, kv_count)
    wide = group * HEAD_SIZE
    big = pl.BlockSpec((rows, wide), lambda g: (0, g + first))
    row = pl.BlockSpec((group, rows), lambda g: (g + first, 0))
    table = pl.BlockSpec((rows, HEAD_SIZE), lambda g: (0, 0))
    pair = pl.BlockSpec((rows, 2 * HEAD_SIZE), lambda g: (0, g))
    one = pl.BlockSpec((rows, HEAD_SIZE), lambda g: (0, g))
    part = pl.BlockSpec((rows, wide), lambda g: (0, g))
    part_row = pl.BlockSpec((group, rows), lambda g: (g, 0))
    return pl.pallas_call(
        functools.partial(diagonal_kernel, group),
        out_shape=[
            jax.ShapeDtypeStruct((rows, count * wide), jnp.bfloat16),
            jax.ShapeDtypeStruct((count * group, rows), jnp.float32),
            jax.ShapeDtypeStruct((rows, count * wide), jnp.bfloat16),
            jax.ShapeDtypeStruct((rows, count * 2 * HEAD_SIZE), jnp.float32),
        ],
        grid=(count,),
        in_specs=[big, big, big, row, table, table, one, one],
        out_specs=[part, part_row, part, pair],
        scratch_shapes=[pltpu.VMEM((rows, group * rows), jnp.bfloat16)] * 2,
        compiler_params=params(1, 60),
        cost_estimate=pl.CostEstimate(
            flops=20 * count * group * rows * rows * HEAD_SIZE,
            bytes_accessed=rows * count * wide * 12,
            transcendentals=0,
        ),
        name="diagonal",
    )(q, do, out, lse, c, s, keys, values)


def part_of(shape, n):
    places, hops, piece, _ = shape
    return pl.BlockSpec(
        (places, None, piece, 2 * HEAD_SIZE),
        lambda g, info, *_: (0, lax.rem(info[0] + hops - n, hops), 0, g),
    )


def cross_kernel(group, joint, final, ours, info_ref, place_ref, anc_ref, rq_ref, do_ref, lse_ref, delta_ref, c_ref, s_ref, dq_in_ref, *refs):
    sets = len(joint)
    refs = list(refs)
    kv_refs = [[refs.pop(0) for _ in range(4 if ours else 1)] for _ in range(sum(joint))]
    if final == 2:
        refs.pop(0)
    dq_ref = refs.pop(0)
    dkv_refs = [refs.pop(0) for _ in range(sum(joint))]
    p_ref, ds_ref, k_ref, v_ref = refs[:4]
    total_ref = refs[4] if sets > 1 else None
    rows = rq_ref.shape[0]
    c, s = c_ref[...] * SCALE, s_ref[...] * SCALE

    def put(cols, total):
        if final and sets == 1:
            dq_ref[:, cols] = turn_back(total, c, s).astype(jnp.bfloat16)
        elif sets == 1:
            dq_ref[:, cols] = total.astype(jnp.bfloat16)
        else:
            total_ref[:, cols] = total

    def run(members, fresh):
        here = slice(0, len(members) * rows)
        for n, m in enumerate(members):
            at = slice(n * rows, (n + 1) * rows)
            if ours:
                raw_ref, values_ref, kc_ref, ks_ref = kv_refs[m]
                raw = raw_ref[...].astype(jnp.float32)
                k_ref[at] = turn(raw, kc_ref[...], ks_ref[...]).astype(jnp.bfloat16)
                v_ref[at] = values_ref[...]
            else:
                both = kv_refs[m][0][...].reshape(rows, 2 * HEAD_SIZE)
                k_ref[at] = both[:, :HEAD_SIZE]
                v_ref[at] = both[:, HEAD_SIZE:]
        k = k_ref[here]
        for h in range(group):
            lanes = slice(h * rows, (h + 1) * rows)
            p_ref[here, lanes], ds_ref[here, lanes] = fronts(
                rq_ref[:, cols_of(h)],
                do_ref[:, cols_of(h)],
                lse_ref[h : h + 1, :] * LOG2E,
                delta_ref[h : h + 1, :],
                k,
                v_ref[here],
            )
        gk = dot(ds_ref[here], stacked(rq_ref, group), NN) * LN2
        gv = dot(p_ref[here], stacked(do_ref, group), NN)
        for n, m in enumerate(members):
            own = slice(n * rows, (n + 1) * rows)
            dkv_refs[m][:, :HEAD_SIZE] = gk[own].astype(jnp.bfloat16)
            dkv_refs[m][:, HEAD_SIZE:] = gv[own].astype(jnp.bfloat16)
        for h in range(group):
            cols = cols_of(h)
            before = dq_in_ref[:, cols].astype(jnp.float32) if fresh else total_ref[:, cols]
            put(cols, before + dot(ds_ref[here, h * rows : (h + 1) * rows], k, TN))

    def skip(members, fresh):
        if fresh:
            for h in range(group):
                put(cols_of(h), dq_in_ref[:, cols_of(h)].astype(jnp.float32))
        for m in members:
            dkv_refs[m][...] = jnp.zeros_like(dkv_refs[m])

    start = 0
    for i, size in enumerate(joint):
        members = tuple(range(start, start + size))
        start += size
        if ours:
            counts = info_ref[0] > i
        else:
            counts = anc_ref[place_ref[info_ref[1]]] >= 0
        pl.when(counts)(functools.partial(run, members, i == 0))
        pl.when(jnp.logical_not(counts))(functools.partial(skip, members, i == 0))
    if sets > 1:
        for h in range(group):
            total = total_ref[:, cols_of(h)]
            if final:
                total = turn_back(total, c, s)
            dq_ref[:, cols_of(h)] = total.astype(jnp.bfloat16)


def cross(kv_count, first, count, tree, ours, joint, rq, do, lse, delta, c, s, dq, kvs, whole=None, final=False):
    rows, width = do.shape
    group = heads_of(width, kv_count)
    wide = group * HEAD_SIZE
    most = max(joint)
    big = pl.BlockSpec((rows, wide), lambda g, *_: (0, g + first))
    row = pl.BlockSpec((group, rows), lambda g, *_: (g + first, 0))
    table = pl.BlockSpec((rows, HEAD_SIZE), lambda g, *_: (0, 0))
    pair = pl.BlockSpec((rows, 2 * HEAD_SIZE), lambda g, *_: (0, g))
    args = [*tree, rq, do, lse, delta, c, s, dq]
    args += [x for x, _ in kvs] if not ours else [y for x, kc, ks in kvs for y in (x, x, kc, ks)]
    in_specs = [big, big, row, row, table, table, big]
    if ours:
        keys_at = pl.BlockSpec((rows, HEAD_SIZE), lambda g, *_: (0, g + first))
        values_at = pl.BlockSpec((rows, HEAD_SIZE), lambda g, *_: (0, g + first + kv_count))
        in_specs += [keys_at, values_at, table, table] * len(kvs)
    else:
        in_specs += [pair if n is None else part_of(x.shape, n) for x, n in kvs]
    mode = 0
    aliases = {}
    if final:
        mode = 1
        if whole is not None:
            mode = 2
            aliases = {len(args): 0}
            args.append(whole)
            in_specs.append(pl.BlockSpec(memory_space=pl.ANY))
    dq_shape = (
        jax.ShapeDtypeStruct((rows, width), jnp.bfloat16)
        if final
        else jax.ShapeDtypeStruct(dq.shape, jnp.bfloat16)
    )
    return pl.pallas_call(
        functools.partial(cross_kernel, group, joint, mode, ours),
        out_shape=[dq_shape]
        + [jax.ShapeDtypeStruct((rows, count * 2 * HEAD_SIZE), jnp.bfloat16)] * len(kvs),
        grid_spec=pltpu.PrefetchScalarGridSpec(
            num_scalar_prefetch=3,
            grid=(count,),
            in_specs=in_specs,
            out_specs=[big] + [pair] * len(kvs),
            scratch_shapes=[pltpu.VMEM((most * rows, group * rows), jnp.bfloat16)] * 2
            + [pltpu.VMEM((most * rows, HEAD_SIZE), jnp.bfloat16)] * 2
            + ([pltpu.VMEM((rows, wide), jnp.float32)] if len(joint) > 1 else []),
        ),
        input_output_aliases=aliases,
        compiler_params=params(1, 60),
        cost_estimate=pl.CostEstimate(
            flops=20 * count * group * rows * rows * HEAD_SIZE * len(kvs),
            bytes_accessed=rows * count * wide * 12,
            transcendentals=0,
        ),
        name="cross",
    )(*args)


def settle_kernel(counts, own_ref, c_ref, s_ref, *refs):
    *in_refs, o_ref = refs
    c, s = c_ref[...], s_ref[...]
    a = 0
    for count in counts:
        mine, in_refs = in_refs[:count], in_refs[count:]
        for b in range(0, mine[0].shape[1], 2 * HEAD_SIZE):
            total = own_ref[:, a : a + 2 * HEAD_SIZE]
            for ref in mine:
                total = total + ref[:, b : b + 2 * HEAD_SIZE].astype(jnp.float32)
            o_ref[:, a : a + HEAD_SIZE] = turn_back(total[:, :HEAD_SIZE], c, s)
            o_ref[:, a + HEAD_SIZE : a + 2 * HEAD_SIZE] = total[:, HEAD_SIZE:]
            a += 2 * HEAD_SIZE


def settle(local, chunks, c, s):
    return pl.pallas_call(
        functools.partial(settle_kernel, [len(x) for x in chunks]),
        out_shape=jax.ShapeDtypeStruct(local.shape, jnp.float32),
        compiler_params=params(0, 12),
        name="settle",
    )(local, c, s, *[x for chunk in chunks for x in chunk])


def finish_kernel(own_ref, children_ref, dk_ref, dv_ref):
    for g in range(dk_ref.shape[1] // HEAD_SIZE):
        a, b = g * HEAD_SIZE, 2 * g * HEAD_SIZE
        total = own_ref[:, b : b + 2 * HEAD_SIZE]
        total = total + children_ref[:, b : b + 2 * HEAD_SIZE].astype(jnp.float32)
        dk_ref[:, a : a + HEAD_SIZE] = total[:, :HEAD_SIZE].astype(jnp.bfloat16)
        dv_ref[:, a : a + HEAD_SIZE] = total[:, HEAD_SIZE:].astype(jnp.bfloat16)


def finish(base, children):
    rows, width = base.shape
    return pl.pallas_call(
        finish_kernel,
        out_shape=[jax.ShapeDtypeStruct((rows, width // 2), jnp.bfloat16)] * 2,
        compiler_params=params(0, 8),
        name="finish",
    )(base, children)


def body(
    queries,
    unrotated_keys,
    value_rows,
    outputs,
    output_gradient,
    saved_logsumexp,
    ancestors,
    placement,
    positions,
):
    hops = lax.axis_size("head")
    places = lax.axis_size("ctx")
    here = lax.axis_index("ctx")
    me = lax.axis_index("head")
    rows = queries.shape[0]
    assert rows * hops == TREE_BLOCK and placement.shape[0] == places
    assert ancestors.shape[1] == 1
    c, s = rope_tables(positions)

    parents = ancestors.reshape(-1)
    tree = (jnp.stack([me, here]).astype(jnp.int32), placement, parents)

    kv_count = unrotated_keys.shape[1] // HEAD_SIZE
    sizes = split(kv_count)
    chunks = range(len(sizes))
    firsts = [sum(sizes[:g]) for g in chunks]

    def exchange(x):
        width = x.shape[-1]
        return lax.all_to_all(
            x.reshape(places, rows // places, width), "ctx", 0, 0, tiled=True
        )

    def shift(x, n, wrap):
        route = [(i, (i + n) % hops) for i in range(hops) if wrap or 0 <= i + n < hops]
        return lax.ppermute(x, "head", route)

    raw = side(unrotated_keys, value_rows)

    piece_rows = rows // places
    offset = me * rows + here * piece_rows + jnp.arange(piece_rows, dtype=jnp.int32)
    middle_at = (TREE_BLOCK * placement[:, None] + offset[None, :]).reshape(-1)
    middle_c, middle_s = [
        t.reshape(places, piece_rows, HEAD_SIZE) for t in rope_tables(middle_at)
    ]

    middle = exchange(raw)
    own_kv = [(shift(raw, n, False), *rope_tables(positions - n * rows)) for n in range(1, hops)]
    rq, delta, dq, local = diagonal(
        queries, output_gradient, outputs, saved_logsumexp, c, s, unrotated_keys, value_rows
    )
    copies = [hops if hops == 2 and g else 1 for g in chunks]
    picked = pick(sizes, copies, placement, parents, middle, middle_c, middle_s)
    near = []
    for g in chunks:
        send = picked[g]
        if g:
            send, near[-1] = lax.optimization_barrier((send, near[-1]))
        if copies[g] == 1:
            near.append(exchange(send))
        else:
            near.append(lax.all_to_all(send, ("ctx", "head"), 0, 0, tiled=True))

    far = []
    for g in chunks:
        if copies[g] == 1:
            at_hand = near[g].reshape(rows, -1)
            far.append([(shift(at_hand, n, True), None) for n in range(1, hops)])
            near[g] = (at_hand, None)
        else:
            both = near[g].reshape(places, hops, piece_rows, -1)
            far.append([(both, n) for n in range(1, hops)])
            near[g] = (both, 0)

    def tiles(g, dq, kvs, ours, joint, whole=None, final=False):
        return cross(
            kv_count, firsts[g], sizes[g], tree, ours, joint, rq, output_gradient,
            saved_logsumexp, delta, c, s, dq, kvs, whole, final,
        )

    grad_queries = None
    ups, backs = [], []
    for g in chunks:

        def peers(part, *rest):
            return tiles(g, part, own_kv, True, (1,) * (hops - 1), *rest)

        def parent(part, *rest):
            return tiles(g, part, [near[g]], False, (1,), *rest)

        def beyond(part, *rest):
            return tiles(g, part, far[g], False, (hops - 1,), *rest)

        if g == 0:
            part, *own_part = peers(dq)
            part, near_part = parent(part)
            grad_queries, *far_part = beyond(part, None, True)
        else:
            part, *far_part = beyond(dq)
            part, near_part = parent(part)
            grad_queries, *own_part = peers(part, grad_queries, True)
        backs.append([shift(x, -n - 1, False) for n, x in enumerate(own_part)])
        joined = [shift(x, -n - 1, True) for n, x in enumerate(far_part)]
        total = near_part.astype(jnp.float32)
        for x in joined:
            total = total + x.astype(jnp.float32)
        send = total.astype(jnp.bfloat16)
        if g:
            send, ups[-1] = lax.optimization_barrier((send, ups[-1]))
        ups.append(exchange(send))
    base = settle(local, backs, c, s)
    merged = merge(placement, parents, middle_c, middle_s, ups)
    children = exchange(merged).reshape(rows, -1)
    grad_keys, grad_values = finish(base, children)
    return (grad_queries, grad_keys, grad_values)


def split(kv_count):
    return (kv_count // 2, kv_count - kv_count // 2)


def solution(mesh):
    return jax.shard_map(
        body,
        mesh=mesh,
        in_specs=(
            P(("ctx", "head"), None),
            P(("ctx", "head"), None),
            P(("ctx", "head"), None),
            P(("ctx", "head"), None),
            P(("ctx", "head"), None),
            P(None, ("ctx", "head")),
            P(),
            P(),
            P(("ctx", "head")),
        ),
        out_specs=(P(("ctx", "head"), None), P(("ctx", "head"), None), P(("ctx", "head"), None)),
        check_vma=False,
    )
```
